256 devices in a mesh: ctx: 32 (over z, x_lo, core), mp: 8 (over y, x_hi).
Axes of the slice: x: 4 (x_hi: 2, x_lo: 2; x = x_hi * 2 + x_lo), y: 4, z: 8, core: 2. Of those that a mesh axis runs over, the one named last changes fastest.
Arguments:
- byte_qkv: bfloat16 [16384, 3, 4096], P('ctx', None, 'mp'), may hold values from -14 to 14
- kv_weight: bfloat16 [4096, 2, 4096], P(None, None, 'mp'), may hold values from -4 to 4
- patch_bounds: int32 [32, 161], replicated, may hold values from 0 to 16384, as said below
Outputs:
- mixed: bfloat16 [5120, 4096], P('ctx', 'mp')
The draws below stay inside these ranges and needn't reach their ends.
Inputs may be any that keep to these rules, and one draw needn't show every extreme that they name: `patch_bounds`: row c lists in increasing order the first bytes of the patches that begin in bytes c * 512 to (c + 1) * 512 - 1, then the end of its last patch, repeated to the end of the row. The patches cover all 16384 bytes, each is 1 to 16 bytes long, one is exactly 16 long, and some row lists exactly 160 patches.
All inputs are finite; a program needn't handle non-finite values.
Results may differ from the reference program's by a relative error of at most 0.002.
The reference program's roundings to bfloat16 on the way count: a program that leaves them out, or rounds other values in their place, can miss the bound.
Values may be sent and summed in bfloat16 or wider, within the bound.
A program may use at most 128 MiB of HBM per device.

```python
import math
import jax
import jax.numpy as jnp
from jax import lax

D = 4096
HEADS = 32
WIN = 16
BYTE_DEV = 512
PCAP = 160
BYTES = 16384
N_CTX = 32


def draw_byte_qkv(key, part):
    base = jax.random.fold_in(key, 29)
    key_noise = jax.random.fold_in(base, 0)
    component = jnp.array([1.0, 1.0, 2.0], jnp.float32)[None, :, None]
    whole = jnp.clip(jax.random.normal(key_noise, (BYTES, 3, D), jnp.float32), -6.0, 6.0) * component
    return whole.astype(jnp.bfloat16)


def draw_kv_weight(key, part):
    base = jax.random.fold_in(key, 5)
    weight_scale = 2.0 / math.sqrt(D)
    whole = jnp.clip(jax.random.normal(base, (D, 2, D), jnp.float32), -6.0, 6.0) * weight_scale
    return whole.astype(jnp.bfloat16)


def draw_patch_bounds(key, part):
    base = jax.random.fold_in(key, 17)
    key_offset, key_counts, key_full, key_order = jax.random.split(base, 4)
    lattice_count = BYTE_DEV // WIN
    offset = jax.random.randint(key_offset, (), 1, WIN)
    device = jnp.arange(N_CTX, dtype=jnp.int32)
    extra_cap = PCAP - lattice_count - (device == 0).astype(jnp.int32)
    extra = jax.random.randint(key_counts, (N_CTX,), 0, extra_cap + 1)
    fullest = jax.random.randint(key_full, (), 0, N_CTX)
    extra = jnp.where(device == fullest, extra_cap, extra)
    position = jnp.arange(BYTE_DEV, dtype=jnp.int32)
    lattice = (position >= offset) & ((position - offset) % WIN == 0)
    reserved = (position < offset + WIN) | (position > offset + BYTE_DEV - WIN)
    free_spot = jnp.logical_not(lattice) & jnp.logical_not(reserved)
    priority = jax.random.permutation(key_order, N_CTX * BYTE_DEV).astype(jnp.int32).reshape(N_CTX, BYTE_DEV)
    ranked = jnp.where(free_spot[None, :], priority, N_CTX * BYTE_DEV)
    cutoff = jnp.take_along_axis(jnp.sort(ranked, axis=1), extra[:, None], axis=1)
    chosen = free_spot[None, :] & (ranked < cutoff)
    first_byte = (device[:, None] == 0) & (position[None, :] == 0)
    is_start = lattice[None, :] | chosen | first_byte
    sort_key = jnp.sort(jnp.where(is_start, position[None, :], 2 * BYTE_DEV), axis=1)[:, :PCAP + 1]
    row_end = jnp.where(device < N_CTX - 1, (device + 1) * BYTE_DEV + offset, N_CTX * BYTE_DEV)
    result = jnp.where(sort_key < BYTE_DEV, device[:, None] * BYTE_DEV + sort_key, row_end[:, None])
    return result.astype(jnp.int32)


def setup_inputs(seed: int = 0) -> dict:
    key_of = jax.random.split(jax.random.key(seed), 4)
    byte_qkv = draw_byte_qkv(jax.random.fold_in(key_of[3], 71), 0)
    kv_weight = draw_kv_weight(jax.random.fold_in(key_of[3], 71), 0)
    patch_bounds = draw_patch_bounds(jax.random.fold_in(key_of[3], 71), 0)
    return dict(byte_qkv=byte_qkv, kv_weight=kv_weight, patch_bounds=patch_bounds)


masked_score = -1e+30

def reference(byte_qkv, kv_weight, patch_bounds):
    slot_total = N_CTX * PCAP
    head_dim = D // HEADS
    score_scale = 1.0 / math.sqrt(head_dim)
    starts = patch_bounds[:, :PCAP].reshape(slot_total)
    lengths = patch_bounds[:, 1:].reshape(slot_total) - starts
    live_slot = lengths > 0
    offsets = jnp.arange(WIN, dtype=jnp.int32)
    byte_index = jnp.clip(starts[:, None] + offsets[None, :], 0, BYTES - 1).astype(jnp.int32)
    inside = offsets[None, :] < lengths[:, None]

    def cross_head(head_index):
        columns = lax.dynamic_slice_in_dim(byte_qkv, head_index * head_dim, head_dim, 2)
        window = columns[byte_index]
        queries = lax.optimization_barrier(jnp.max(jnp.where(inside[:, :, None], window[:, :, 0], -jnp.inf), axis=1))
        queries = jnp.where(live_slot[:, None], queries, 0).astype(jnp.bfloat16)
        scores = jnp.einsum('sd,swd->sw', queries.astype(jnp.float32), window[:, :, 1].astype(jnp.float32)) * score_scale
        scores = jnp.where(inside, scores, masked_score)
        scores = scores - lax.optimization_barrier(jnp.max(scores, axis=1, keepdims=True))
        exp_terms = jnp.exp(scores)
        weights = (exp_terms / lax.optimization_barrier(jnp.sum(exp_terms, axis=1, keepdims=True))).astype(jnp.bfloat16)
        pooled = jnp.einsum('sw,swd->sd', weights.astype(jnp.float32), window[:, :, 2].astype(jnp.float32))
        return jnp.where(live_slot[:, None], pooled, 0.0).astype(jnp.bfloat16)
    heads_out = lax.map(cross_head, jnp.arange(HEADS, dtype=jnp.int32))
    patch_state = heads_out.transpose(1, 0, 2).reshape(slot_total, D)
    key_part = jnp.dot(patch_state, kv_weight[:, 0, :], preferred_element_type=jnp.float32).astype(jnp.bfloat16)
    value_part = jnp.dot(patch_state, kv_weight[:, 1, :], preferred_element_type=jnp.float32).astype(jnp.bfloat16)
    slot_order = jnp.arange(slot_total, dtype=jnp.int32)
    visible = (slot_order[None, :] <= slot_order[:, None]) & live_slot[None, :]

    def global_head(head_index):
        query_cols = lax.dynamic_slice_in_dim(patch_state, head_index * head_dim, head_dim, 1)
        key_cols = lax.dynamic_slice_in_dim(key_part, head_index * head_dim, head_dim, 1)
        value_cols = lax.dynamic_slice_in_dim(value_part, head_index * head_dim, head_dim, 1)
        scores = jnp.dot(query_cols, key_cols.T, preferred_element_type=jnp.float32) * score_scale
        scores = jnp.where(visible, scores, masked_score)
        scores = scores - lax.optimization_barrier(jnp.max(scores, axis=1, keepdims=True))
        exp_terms = jnp.where(visible, jnp.exp(scores), 0.0)
        weights = exp_terms / lax.optimization_barrier(jnp.sum(exp_terms, axis=1, keepdims=True))
        result = jnp.dot(weights, value_cols.astype(jnp.float32), precision=lax.Precision.HIGHEST)
        return jnp.where(live_slot[:, None], result, 0.0)
    attended = lax.map(global_head, jnp.arange(HEADS, dtype=jnp.int32))
    attended = attended.transpose(1, 0, 2).reshape(slot_total, D)
    return (patch_state.astype(jnp.float32) + attended).astype(jnp.bfloat16)
```

```python
import functools
import math

import jax
import jax.numpy as jnp
from jax import lax
from jax.experimental import pallas as pl
from jax.experimental.pallas import tpu as pltpu
from jax.sharding import PartitionSpec as P

D = 4096
HEADS = 32
WIN = 16
HD = 128
BYTE_DEV = 512
EXT = BYTE_DEV + WIN
PCAP = 160
COLS = 512
HERE = 4
N_MP = 8
N_Z = 8
GROUP = 4
ROWS = GROUP * PCAP
SCALE = 1.0 / math.sqrt(HD)
MASKED = -1e30
F32 = jnp.float32
BF16 = jnp.bfloat16
MESH = pl.DeviceIdType.MESH


def cross_body(bounds_ref, bytes_ref, edge_ref, out_ref, ext):
    c = lax.axis_index("ctx")
    row = bounds_ref[pl.ds(c, 1), :] - c * BYTE_DEV
    starts = row[:, :PCAP]
    ends = row[:, 1 : PCAP + 1]
    diag = lax.broadcasted_iota(jnp.int32, (PCAP, PCAP), 0) == lax.broadcasted_iota(
        jnp.int32, (PCAP, PCAP), 1
    )
    start_col = jnp.sum(jnp.where(diag, starts, 0), axis=1, keepdims=True)
    end_col = jnp.sum(jnp.where(diag, ends, 0), axis=1, keepdims=True)
    byte_row = lax.broadcasted_iota(jnp.int32, (PCAP, EXT), 1)
    inside = (byte_row >= start_col) & (byte_row < end_col)
    first = ((byte_row == start_col) & (end_col > start_col)).astype(F32).astype(BF16)
    byte_col = lax.broadcasted_iota(jnp.int32, (EXT, PCAP), 0)
    inside_t = (byte_col >= starts) & (byte_col < ends)
    left = jnp.sum(jnp.where(inside_t, ends - byte_col, 0), axis=1, keepdims=True)
    for part in range(3):
        ext[part, 0:BYTE_DEV, :] = bytes_ref[part]
        ext[part, BYTE_DEV:EXT, :] = edge_ref[part]
    for h in range(HERE):
        cols = slice(h * HD, (h + 1) * HD)
        top = ext[0, :, cols].astype(F32)
        for shift in (1, 2, 4, 8):
            later = pltpu.roll(top, EXT - shift, 0)
            top = jnp.maximum(top, jnp.where(left > shift, later, -jnp.inf))
        query = jnp.dot(first, top.astype(BF16), preferred_element_type=F32).astype(BF16)
        scores = (
            lax.dot_general(
                query, ext[1, :, cols], (((1,), (1,)), ((), ())), preferred_element_type=F32
            )
            * SCALE
        )
        scores = jnp.where(inside, scores, MASKED)
        scores = scores - jnp.max(scores, axis=1, keepdims=True)
        exp_terms = jnp.where(inside, jnp.exp(scores), 0.0)
        total = jnp.sum(exp_terms, axis=1, keepdims=True)
        weights = (exp_terms / jnp.where(total > 0, total, 1.0)).astype(BF16)
        out_ref[:, cols] = jnp.dot(weights, ext[2, :, cols], preferred_element_type=F32).astype(BF16)


def cross(bounds, bytes3, edge):
    vmem = pl.BlockSpec(memory_space=pltpu.VMEM)
    return pl.pallas_call(
        cross_body,
        out_shape=jax.ShapeDtypeStruct((PCAP, COLS), BF16),
        in_specs=[vmem, vmem, vmem],
        out_specs=vmem,
        scratch_shapes=[pltpu.VMEM((3, EXT, COLS), BF16)],
        compiler_params=pltpu.CompilerParams(vmem_limit_bytes=16 * 2**20),
        name="cross",
    )(bounds, bytes3, edge)


def remote(src, dst, send, recv, where):
    return pltpu.make_async_remote_copy(
        src_ref=src, dst_ref=dst, send_sem=send, recv_sem=recv, device_id=where, device_id_type=MESH
    )


def global_body(
    bounds_ref, state_ref, weight_hbm, out_ref,
    weight, states, acc, kv_own, kv, queries, live, top, sums, mixed,
    w_sem, mp_send, mp_recv, q_send, q_recv, g_send, g_recv, up_send, up_recv, dn_send, dn_recv,
    o_send, o_recv,
):
    ctx = lax.axis_index("ctx")
    mp = lax.axis_index("mp")
    z = ctx // GROUP
    member = ctx % GROUP
    y = mp // 2
    xh = mp % 2

    def at_mp(yy, xx):
        return lax.rem(yy + 4, 4) * 2 + xx

    def mate(k):
        return z * GROUP + lax.rem(member + k, GROUP)

    y_up, y_dn, x_other = at_mp(y + 1, xh), at_mp(y - 1, xh), at_mp(y, 1 - xh)
    z_up = lax.rem(z + 1, N_Z) * GROUP + member
    z_dn = lax.rem(z + N_Z - 1, N_Z) * GROUP + member

    w_copy = pltpu.make_async_copy(weight_hbm, weight, w_sem)
    w_copy.start()

    barrier = pltpu.get_barrier_semaphore()
    partners = [{"ctx": ctx, "mp": y_up}, {"ctx": ctx, "mp": y_dn}, {"ctx": ctx, "mp": x_other},
                {"ctx": z_up, "mp": mp}, {"ctx": z_dn, "mp": mp}]
    partners += [{"ctx": mate(k), "mp": mp} for k in range(1, GROUP)]
    for partner in partners:
        pl.semaphore_signal(barrier, inc=1, device_id=partner, device_id_type=MESH)
    pl.semaphore_wait(barrier, len(partners))

    half = PCAP // 2
    lower, upper = pl.ds(0, half), pl.ds(half, half)
    whole = pl.ds(0, PCAP)

    def hand(src, block, rows, slot, to):
        return remote(src, states.at[block, rows], mp_send.at[slot], mp_recv.at[slot], {"ctx": ctx, "mp": to})

    own_x = hand(state_ref, mp, whole, 0, x_other)
    own_up = hand(state_ref, mp, whole, 1, y_up)
    own_dn = hand(state_ref, mp, whole, 2, y_dn)
    own_x.start()
    own_up.start()
    own_dn.start()
    states[mp] = state_ref[...]

    q_copies = []
    for k in range(1, GROUP):
        head = lax.rem(member + k, GROUP)
        copy = remote(
            state_ref.at[:, pl.ds(pl.multiple_of(head * HD, HD), HD)],
            queries.at[pl.ds(pl.multiple_of(member * PCAP, PCAP), PCAP)],
            q_send.at[k - 1], q_recv.at[k - 1], {"ctx": mate(k), "mp": mp},
        )
        copy.start()
        q_copies.append(copy)
    queries[pl.ds(pl.multiple_of(member * PCAP, PCAP), PCAP), :] = state_ref[
        :, pl.ds(pl.multiple_of(member * HD, HD), HD)
    ]

    w_copy.wait()

    def project(block, first=False):
        left = states[block]
        for n in range(4):
            rows = pl.ds(pl.multiple_of(block * COLS, COLS), COLS)
            right = weight[rows, :, n * HD : (n + 1) * HD]
            part = jnp.dot(left, right.reshape(COLS, 2 * HD), preferred_element_type=F32)
            cols = slice(n * 2 * HD, (n + 1) * 2 * HD)
            if first:
                acc[:, cols] = part
            else:
                acc[:, cols] += part

    project(mp, True)

    def arrived(block, rows, slot):
        hand(states.at[block, rows], block, rows, slot, y_up).wait_recv()

    far = at_mp(y + 2, xh)
    arrived(y_dn, whole, 1)
    fwd_up = hand(states.at[y_dn, lower], y_dn, lower, 3, y_up)
    fwd_up.start()
    arrived(y_up, whole, 2)
    fwd_dn = hand(states.at[y_up, upper], y_up, upper, 4, y_dn)
    fwd_dn.start()
    arrived(x_other, whole, 0)
    ox_up = hand(states.at[x_other], x_other, whole, 5, y_up)
    ox_dn = hand(states.at[x_other], x_other, whole, 6, y_dn)
    ox_up.start()
    ox_dn.start()
    project(y_dn)
    project(y_up)
    project(x_other)
    arrived(far, lower, 3)
    arrived(far, upper, 4)
    project(far)
    o_dn, o_up, o_far = at_mp(y - 1, 1 - xh), at_mp(y + 1, 1 - xh), at_mp(y + 2, 1 - xh)
    arrived(o_dn, whole, 5)
    ofwd_up = hand(states.at[o_dn, lower], o_dn, lower, 7, y_up)
    ofwd_up.start()
    arrived(o_up, whole, 6)
    ofwd_dn = hand(states.at[o_up, upper], o_up, upper, 8, y_dn)
    ofwd_dn.start()
    project(o_dn)
    project(o_up)
    arrived(o_far, lower, 7)
    arrived(o_far, upper, 8)
    project(o_far)

    mine = pl.ds(pl.multiple_of(member * PCAP, PCAP), PCAP)
    for n in range(HERE):
        for part in range(2):
            begin = n * 2 * HD + part * HD
            kv_own[part, n] = acc[:, begin : begin + HD].astype(BF16)
    g_copies = []
    for part in range(2):
        for k in range(1, GROUP):
            head = lax.rem(member + k, GROUP)
            slot = part * 3 + k - 1
            copy = remote(
                kv_own.at[part, head], kv.at[z, part, mine], g_send.at[slot], g_recv.at[slot],
                {"ctx": mate(k), "mp": mp},
            )
            copy.start()
            g_copies.append(copy)
        kv[z, part, mine, :] = kv_own[part, member]

    def ring(block, part, slot, up):
        block = lax.rem(block + N_Z, N_Z)
        send, recv, to = (up_send, up_recv, z_up) if up else (dn_send, dn_recv, z_dn)
        return remote(
            kv.at[block, part], kv.at[block, part], send.at[slot], recv.at[slot], {"ctx": to, "mp": mp}
        )

    ring_copies = []

    def send(block, part, slot, up):
        copy = ring(block, part, slot, up)
        copy.start()
        ring_copies.append(copy)

    for part in range(2):
        for k in range(3):
            g_copies[part * 3 + k].wait_recv()
        send(z, part, part, True)
        send(z, part, part, False)

    for copy in q_copies:
        copy.wait_recv()

    bounds = bounds_ref[...]
    alive = bounds[:, 1 : PCAP + 1] > bounds[:, :PCAP]
    live[...] = jnp.where(alive, 0.0, MASKED)

    def bias_of(block):
        rows = [live[pl.ds(block * GROUP + i, 1), :] for i in range(GROUP)]
        return jnp.concatenate(rows, axis=1)

    STEP = PCAP

    def attend(block, start):
        bias = bias_of(block)
        keys = kv[block, 0]
        values = kv[block, 1]

        def chunk(i, _):
            rows = pl.ds(pl.multiple_of(i * STEP, STEP), STEP)
            query = queries[rows, :]
            scores = lax.dot_general(
                query, keys, (((1,), (1,)), ((), ())), preferred_element_type=F32
            ) * SCALE + bias
            if start:
                key_at = lax.broadcasted_iota(jnp.int32, (STEP, ROWS), 1)
                query_at = lax.broadcasted_iota(jnp.int32, (STEP, ROWS), 0) + i * STEP
                scores = jnp.where(key_at <= query_at, scores, MASKED)
            best = jnp.max(scores, axis=1, keepdims=True)
            if not start:
                before = top[rows, :]
                best = jnp.maximum(best, before)
                keep = jnp.exp(before - best)
            weights = jnp.exp(scores - best)
            total = jnp.sum(weights, axis=1, keepdims=True)
            part = jnp.dot(weights.astype(BF16), values, preferred_element_type=F32)
            if start:
                sums[rows, :] = total
                mixed[rows, :] = part
            else:
                sums[rows, :] = sums[rows, :] * keep + total
                mixed[rows, :] = mixed[rows, :] * keep + part
            top[rows, :] = best
            return 0

        lax.fori_loop(0, ROWS // STEP, chunk, 0)

    attend(z, True)

    for hop in range(1, 5):
        for part in range(2):
            for up in (True, False):
                block = z - hop if up else z + hop
                if hop == 4 and part == (1 if up else 0):
                    continue
                slot = 2 * (hop - 1) + part if hop < 4 else 6
                ring(block, part, slot, up).wait_recv()
                if hop < 3:
                    send(block, part, 2 * hop + part, up)
                elif hop == 3 and part == (0 if up else 1):
                    send(block, part, 6, up)
        blocks = (z - hop, z + hop) if hop < 4 else (z - hop,)
        for block in blocks:
            index = lax.rem(block + N_Z, N_Z)

            @pl.when(index < z)
            def _():
                attend(index, False)

    bounds_z = [live[pl.ds(z * GROUP + i, 1), :] for i in range(GROUP)]
    eye = lax.broadcasted_iota(jnp.int32, (PCAP, PCAP), 0) == lax.broadcasted_iota(
        jnp.int32, (PCAP, PCAP), 1
    )
    for copy in g_copies:
        copy.wait_send()
    o_copies = []
    for i in range(GROUP):
        rows = pl.ds(i * PCAP, PCAP)
        dead = jnp.sum(jnp.where(eye, bounds_z[i], 0.0), axis=1, keepdims=True)
        value = jnp.where(dead < 0, 0.0, mixed[rows, :] / sums[rows, :])
        value = queries[rows, :].astype(F32) + value
        kv_own[0, i] = value.astype(BF16)
    column = pl.ds(pl.multiple_of(member * HD, HD), HD)
    for k in range(1, GROUP):
        index = lax.rem(member + k, GROUP)
        copy = remote(
            kv_own.at[0, index], out_ref.at[:, column], o_send.at[k - 1], o_recv.at[k - 1],
            {"ctx": mate(k), "mp": mp},
        )
        copy.start()
        o_copies.append(copy)
    out_ref[:, column] = kv_own[0, member]
    for copy in o_copies:
        copy.wait_recv()
    for copy in o_copies + q_copies + ring_copies + [own_x, own_up, own_dn, fwd_up, fwd_dn, ox_up, ox_dn, ofwd_up, ofwd_dn]:
        copy.wait_send()


def globally(bounds, state, weight):
    vmem = pl.BlockSpec(memory_space=pltpu.VMEM)
    dma = pltpu.SemaphoreType.DMA
    return pl.pallas_call(
        global_body,
        out_shape=jax.ShapeDtypeStruct((PCAP, COLS), BF16),
        in_specs=[vmem, vmem, pl.BlockSpec(memory_space=pl.ANY)],
        out_specs=vmem,
        scratch_shapes=[
            pltpu.VMEM((D, 2, COLS), BF16),
            pltpu.VMEM((N_MP, PCAP, COLS), BF16),
            pltpu.VMEM((PCAP, 2 * COLS), F32),
            pltpu.VMEM((2, HERE, PCAP, HD), BF16),
            pltpu.VMEM((N_Z, 2, ROWS, HD), BF16),
            pltpu.VMEM((ROWS, HD), BF16),
            pltpu.VMEM((32, PCAP), F32),
            pltpu.VMEM((ROWS, 1), F32),
            pltpu.VMEM((ROWS, 1), F32),
            pltpu.VMEM((ROWS, HD), F32),
            dma, dma((9,)), dma((9,)), dma((3,)), dma((3,)), dma((6,)), dma((6,)),
            dma((7,)), dma((7,)), dma((7,)), dma((7,)), dma((3,)), dma((3,)),
        ],
        compiler_params=pltpu.CompilerParams(
            vmem_limit_bytes=48 * 2**20, collective_id=0, has_side_effects=True
        ),
        name="globally",
    )(bounds, state, weight)


def shards(byte_qkv, kv_weight, patch_bounds):
    bytes3 = byte_qkv.transpose(1, 0, 2)
    count = lax.axis_size("ctx")
    edge = lax.ppermute(bytes3[:, :WIN], "ctx", [(i, i - 1) for i in range(1, count)])
    state = cross(patch_bounds, bytes3, edge)
    return globally(patch_bounds, state, kv_weight)


def solution(mesh):
    return jax.shard_map(
        shards,
        mesh=mesh,
        in_specs=(P("ctx", None, "mp"), P(None, None, "mp"), P()),
        out_specs=P("ctx", "mp"),
        check_vma=False,
    )
```

```python
import math

import jax
import jax.numpy as jnp
from jax import lax
from jax.experimental import pallas as pl
from jax.experimental.pallas import tpu as pltpu
from jax.sharding import PartitionSpec as P

D = 4096
HEADS = 32
WIN = 16
HD = 128
BYTE_DEV = 512
EXT = BYTE_DEV + WIN
PCAP = 160
COLS = 512
HERE = 4
N_MP = 8
N_Z = 8
GROUP = 4
ROWS = GROUP * PCAP
SCALE = 1.0 / math.sqrt(HD)
SCALE2 = SCALE * math.log2(math.e)
EDGE = BYTE_DEV - 2 * WIN
MASKED = -1e30
F32 = jnp.float32
BF16 = jnp.bfloat16
CHUNKS = ((0, 64), (64, 96))
MESH = pl.DeviceIdType.MESH


def remote(src, dst, send, recv, where):
    return pltpu.make_async_remote_copy(
        src_ref=src, dst_ref=dst, send_sem=send, recv_sem=recv, device_id=where, device_id_type=MESH
    )


def kernel(
    bounds_hbm, bytes_hbm, weight_hbm, out_ref,
    bounds_ref, ext, tops, state, weight, plain, states, acc, own0, own1, kv0, kv1,
    queries, live, bias0, bias1, top, mixed, outgoing,
    in_sem, halo_send, halo_recv, mp_send, mp_recv, q_send, q_recv, g_send, g_recv,
    up_send, up_recv, dn_send, dn_recv, o_send, o_recv,
):
    ctx = lax.axis_index("ctx")
    mp = lax.axis_index("mp")
    z = ctx // GROUP
    member = ctx % GROUP
    y = mp // 2
    xh = mp % 2
    owns, kvs, biases = (own0, own1), (kv0, kv1), (bias0, bias1)
    sent = []

    def at_mp(yy, xx):
        return lax.rem(yy + 4, 4) * 2 + xx

    def mate(k):
        return z * GROUP + lax.rem(member + k, GROUP)

    y_up, y_dn, x_other = at_mp(y + 1, xh), at_mp(y - 1, xh), at_mp(y, 1 - xh)
    far = at_mp(y + 2, xh)
    o_dn, o_up, o_far = at_mp(y - 1, 1 - xh), at_mp(y + 1, 1 - xh), at_mp(y + 2, 1 - xh)
    z_up = lax.rem(z + 1, N_Z) * GROUP + member
    z_dn = lax.rem(z + N_Z - 1, N_Z) * GROUP + member
    before_me = lax.rem(ctx + N_Z * GROUP - 1, N_Z * GROUP)
    after_me = lax.rem(ctx + 1, N_Z * GROUP)

    bounds_in = pltpu.make_async_copy(bounds_hbm, bounds_ref, in_sem.at[0])
    bytes_in = pltpu.make_async_copy(bytes_hbm, ext.at[:, pl.ds(0, BYTE_DEV)], in_sem.at[1])
    weight_in = pltpu.make_async_copy(weight_hbm, weight, in_sem.at[2])
    bounds_in.start()
    bytes_in.start()
    weight_in.start()

    barrier = pltpu.get_barrier_semaphore()
    partners = [{"ctx": before_me, "mp": mp}, {"ctx": after_me, "mp": mp},
                {"ctx": ctx, "mp": y_up}, {"ctx": ctx, "mp": y_dn}, {"ctx": ctx, "mp": x_other},
                {"ctx": z_up, "mp": mp}, {"ctx": z_dn, "mp": mp}]
    partners += [{"ctx": mate(k), "mp": mp} for k in range(1, GROUP)]
    for partner in partners:
        pl.semaphore_signal(barrier, inc=1, device_id=partner, device_id_type=MESH)
    pl.semaphore_wait(barrier, len(partners))

    halo = remote(
        bytes_hbm.at[:, pl.ds(0, WIN)], ext.at[:, pl.ds(BYTE_DEV, WIN)], halo_send, halo_recv,
        {"ctx": before_me, "mp": mp},
    )
    halo.start()
    sent.append(halo)

    bounds_in.wait()
    row = bounds_ref[pl.ds(ctx, 1), :] - ctx * BYTE_DEV
    starts = row[:, :PCAP]
    ends = row[:, 1 : PCAP + 1]
    diag = lax.broadcasted_iota(jnp.int32, (PCAP, PCAP), 0) == lax.broadcasted_iota(
        jnp.int32, (PCAP, PCAP), 1
    )
    start_col = jnp.sum(jnp.where(diag, starts, 0), axis=1, keepdims=True)
    end_col = jnp.sum(jnp.where(diag, ends, 0), axis=1, keepdims=True)
    byte_col = lax.broadcasted_iota(jnp.int32, (EXT, PCAP), 0)
    inside_t = (byte_col >= starts) & (byte_col < ends)
    left = jnp.sum(jnp.where(inside_t, ends - byte_col, 0), axis=1, keepdims=True)

    def patch_tops(begin, end):
        room = left[begin:end]
        for h in range(HERE):
            cols = slice(h * HD, (h + 1) * HD)
            best = ext[0, begin:end, cols].astype(F32)
            for shift in (1, 2, 4, 8):
                later = pltpu.roll(best, end - begin - shift, 0)
                best = jnp.maximum(best, jnp.where(room > shift, later, -jnp.inf))
            tops[begin:end, cols] = best.astype(BF16)

    bytes_in.wait()
    patch_tops(0, BYTE_DEV)
    halo.wait_recv()
    patch_tops(EDGE, EXT)

    def cross(off, count):
        begin, end = start_col[off : off + count], end_col[off : off + count]
        byte_row = lax.broadcasted_iota(jnp.int32, (count, EXT), 1)
        inside = (byte_row >= begin) & (byte_row < end)
        first = ((byte_row == begin) & (end > begin)).astype(F32).astype(BF16)
        for h in range(HERE):
            cols = slice(h * HD, (h + 1) * HD)
            query = jnp.dot(first, tops[:, cols], preferred_element_type=F32).astype(BF16)
            scores = (
                lax.dot_general(
                    query, ext[1, :, cols], (((1,), (1,)), ((), ())), preferred_element_type=F32
                )
                * SCALE
            )
            scores = jnp.where(inside, scores, MASKED)
            scores = scores - jnp.max(scores, axis=1, keepdims=True)
            terms = jnp.where(inside, jnp.exp(scores), 0.0)
            total = jnp.sum(terms, axis=1, keepdims=True)
            weights = (terms / jnp.where(total > 0, total, 1.0)).astype(BF16)
            state[off : off + count, cols] = jnp.dot(
                weights, ext[2, :, cols], preferred_element_type=F32
            ).astype(BF16)

    def rows_of(c, part=None):
        off, count = CHUNKS[c]
        if part is None:
            return pl.ds(off, count)
        return pl.ds(off + part * (count // 2), count // 2)

    def hand(c, src, block, rows, slot, to):
        slot = 9 * c + slot
        return remote(src, states.at[block, rows], mp_send.at[slot], mp_recv.at[slot], {"ctx": ctx, "mp": to})

    def pass_on(c, block, part, slot, to, own=False):
        rows = rows_of(c, part)
        src = state.at[rows] if own else states.at[block, rows]
        copy = hand(c, src, block, rows, slot, to)
        copy.start()
        sent.append(copy)

    def arrived(c, block, part, slot):
        rows = rows_of(c, part)
        hand(c, states.at[block, rows], block, rows, slot, y_up).wait_recv()

    def send_own(c):
        pass_on(c, mp, None, 0, x_other, True)
        pass_on(c, mp, None, 1, y_up, True)
        pass_on(c, mp, None, 2, y_dn, True)

    def near(c):
        arrived(c, y_dn, None, 1)
        pass_on(c, y_dn, 0, 3, y_up)
        arrived(c, y_up, None, 2)
        pass_on(c, y_up, 1, 4, y_dn)

    def across(c):
        arrived(c, x_other, None, 0)
        pass_on(c, x_other, None, 5, y_up)
        pass_on(c, x_other, None, 6, y_dn)

    def across_near(c):
        arrived(c, o_dn, None, 5)
        pass_on(c, o_dn, 0, 7, y_up)
        arrived(c, o_up, None, 6)
        pass_on(c, o_up, 1, 8, y_dn)

    def prepare(block):
        rows = pl.ds(pl.multiple_of(block * COLS, COLS), COLS)
        plain[block] = weight[rows].reshape(COLS, 2 * COLS)

    def project(c, block, first=False):
        rows = rows_of(c)
        part_rows = (state if first else states.at[block])[rows, :]
        part = jnp.dot(part_rows, plain[block], preferred_element_type=F32)
        if first:
            acc[rows, :] = part
        else:
            acc[rows, :] += part

    def exchange(c):
        off, count = CHUNKS[c]
        own, kv = owns[c], kvs[c]
        mine = pl.ds(pl.multiple_of(member * count, count), count)
        for part in range(2):
            for n in range(HERE):
                begin = part * COLS + n * HD
                own[part, n] = acc[off : off + count, begin : begin + HD].astype(BF16)
        copies = []
        for part in range(2):
            for k in range(1, GROUP):
                slot = 6 * c + part * 3 + k - 1
                copy = remote(
                    own.at[part, lax.rem(member + k, GROUP)], kv.at[z, part, mine],
                    g_send.at[slot], g_recv.at[slot], {"ctx": mate(k), "mp": mp},
                )
                copy.start()
                copies.append(copy)
                sent.append(copy)
            kv[z, part, mine, :] = own[part, member]
        return copies

    def piece(c, block, part, slot, up):
        block = lax.rem(block + N_Z, N_Z)
        slot = 7 * c + slot
        send, recv, to = (up_send, up_recv, z_up) if up else (dn_send, dn_recv, z_dn)
        ref = kvs[c].at[block, part]
        return remote(ref, ref, send.at[slot], recv.at[slot], {"ctx": to, "mp": mp})

    def ring_send(c, block, part, slot, up):
        copy = piece(c, block, part, slot, up)
        copy.start()
        sent.append(copy)

    def ring_start(c, copies):
        for part in range(2):
            for k in range(3):
                copies[part * 3 + k].wait_recv()
            ring_send(c, z, part, part, True)
            ring_send(c, z, part, part, False)

    def ring_hop(c, hop):
        for part in range(2):
            for up in (True, False):
                block = z - hop if up else z + hop
                if hop == 4 and part == (1 if up else 0):
                    continue
                slot = 2 * (hop - 1) + part if hop < 4 else 6
                piece(c, block, part, slot, up).wait_recv()
                if hop < 3:
                    ring_send(c, block, part, 2 * hop + part, up)
                elif hop == 3 and part == (0 if up else 1):
                    ring_send(c, block, part, 6, up)

    def attend(c, block, own):
        off, count = CHUNKS[c]
        keys_here = GROUP * count
        start = own and c == 0
        bias = biases[c][pl.ds(block, 1), :]
        keys = kvs[c][block, 0]
        values = jnp.concatenate([kvs[c][block, 1], jnp.ones((keys_here, HD), BF16)], axis=1)
        for i in range(GROUP):
            rows = slice(i * PCAP, (i + 1) * PCAP)
            scores = lax.dot_general(
                queries[rows, :], keys, (((1,), (1,)), ((), ())), preferred_element_type=F32
            ) + bias
            if own:
                at = lax.broadcasted_iota(jnp.int32, (1, keys_here), 1)
                slot = at + off
                for m in range(1, GROUP):
                    slot = slot + jnp.where(at >= m * count, PCAP - count, 0)
                query_at = lax.broadcasted_iota(jnp.int32, (PCAP, keys_here), 0) + i * PCAP
                scores = jnp.where(slot <= query_at, scores, MASKED)
            best = jnp.max(scores, axis=1, keepdims=True)
            if not start:
                before = top[rows, :]
                best = jnp.maximum(best, before)
                keep = jnp.exp2((before - best) * SCALE2)
            weights = jnp.exp2((scores - best) * SCALE2)
            part = jnp.dot(weights.astype(BF16), values, preferred_element_type=F32)
            if not start:
                part = mixed[rows, :] * keep + part
            mixed[rows, :] = part
            top[rows, :] = best

    def attend_hop(c, hop):
        def one(d, _):
            index = lax.rem(z + (2 * d - 1) * hop + N_Z, N_Z)

            @pl.when(index < z)
            def _():
                attend(c, index, False)

            return 0

        lax.fori_loop(0, 2 if hop < 4 else 1, one, 0)

    cross(*CHUNKS[0])
    send_own(0)
    cross(*CHUNKS[1])
    send_own(1)
    own_rows = pl.ds(pl.multiple_of(member * PCAP, PCAP), PCAP)
    q_copies = []
    for k in range(1, GROUP):
        head = lax.rem(member + k, GROUP)
        copy = remote(
            state.at[:, pl.ds(pl.multiple_of(head * HD, HD), HD)], queries.at[own_rows],
            q_send.at[k - 1], q_recv.at[k - 1], {"ctx": mate(k), "mp": mp},
        )
        copy.start()
        q_copies.append(copy)
        sent.append(copy)
    queries[own_rows, :] = state[:, pl.ds(pl.multiple_of(member * HD, HD), HD)]

    weight_in.wait()
    near(0)
    prepare(mp)
    project(0, mp, True)
    prepare(y_dn)
    project(0, y_dn)
    prepare(y_up)
    project(0, y_up)
    across(0)
    near(1)
    for block in (x_other, far, o_dn, o_up, o_far):
        prepare(block)
    project(0, x_other)
    arrived(0, far, 0, 3)
    arrived(0, far, 1, 4)
    project(0, far)
    across_near(0)
    project(0, o_dn)
    project(0, o_up)
    across(1)
    arrived(0, o_far, 0, 7)
    arrived(0, o_far, 1, 8)
    project(0, o_far)
    g0 = exchange(0)

    bounds = bounds_ref[...]
    live[...] = jnp.where(bounds[:, 1 : PCAP + 1] > bounds[:, :PCAP], 0.0, MASKED)
    for c, (off, count) in enumerate(CHUNKS):
        for block in range(N_Z):
            biases[c][block : block + 1, :] = jnp.concatenate(
                [live[block * GROUP + i : block * GROUP + i + 1, off : off + count] for i in range(GROUP)],
                axis=1,
            )
    project(1, mp, True)
    project(1, y_dn)
    ring_start(0, g0)
    project(1, y_up)
    arrived(1, far, 0, 3)
    arrived(1, far, 1, 4)
    project(1, far)
    project(1, x_other)
    for copy in q_copies:
        copy.wait_recv()
    attend(0, z, True)
    across_near(1)
    project(1, o_dn)
    project(1, o_up)
    ring_hop(0, 1)
    arrived(1, o_far, 0, 7)
    arrived(1, o_far, 1, 8)
    project(1, o_far)
    g1 = exchange(1)
    attend_hop(0, 1)
    ring_hop(0, 2)
    ring_start(1, g1)
    attend(1, z, True)
    attend_hop(0, 2)
    ring_hop(0, 3)
    attend_hop(0, 3)
    ring_hop(1, 1)
    ring_hop(0, 4)
    attend_hop(0, 4)
    attend_hop(1, 1)
    for hop in range(2, 5):
        ring_hop(1, hop)
        attend_hop(1, hop)

    column = pl.ds(pl.multiple_of(member * HD, HD), HD)
    o_copies = []
    for k in (2, 1, 3, 0):
        index = lax.rem(member + k, GROUP)
        rows = pl.ds(pl.multiple_of(index * PCAP, PCAP), PCAP)
        dead = jnp.sum(jnp.where(diag, live[pl.ds(z * GROUP + index, 1), :], 0.0), axis=1, keepdims=True)
        value = jnp.where(dead < 0, 0.0, mixed[rows, :HD] / mixed[rows, HD:])
        outgoing[k] = (queries[rows, :].astype(F32) + value).astype(BF16)
        if k:
            copy = remote(
                outgoing.at[k], out_ref.at[:, column], o_send.at[k - 1], o_recv.at[k - 1],
                {"ctx": mate(k), "mp": mp},
            )
            copy.start()
            o_copies.append(copy)
            sent.append(copy)
    out_ref[:, column] = outgoing[0]
    for copy in o_copies:
        copy.wait_recv()
    for copy in sent:
        copy.wait_send()


def shards(byte_qkv, kv_weight, patch_bounds):
    anywhere = pl.BlockSpec(memory_space=pltpu.HBM)
    dma = pltpu.SemaphoreType.DMA
    (_, n0), (_, n1) = CHUNKS
    return pl.pallas_call(
        kernel,
        out_shape=jax.ShapeDtypeStruct((PCAP, COLS), BF16),
        in_specs=[anywhere, anywhere, anywhere],
        out_specs=pl.BlockSpec(memory_space=pltpu.VMEM),
        scratch_shapes=[
            pltpu.VMEM((32, PCAP + 1), jnp.int32),
            pltpu.VMEM((3, EXT, COLS), BF16),
            pltpu.VMEM((EXT, COLS), BF16),
            pltpu.VMEM((PCAP, COLS), BF16),
            pltpu.VMEM((D, 2, COLS), BF16),
            pltpu.VMEM((N_MP, COLS, 2 * COLS), BF16),
            pltpu.VMEM((N_MP, PCAP, COLS), BF16),
            pltpu.VMEM((PCAP, 2 * COLS), F32),
            pltpu.VMEM((2, HERE, n0, HD), BF16),
            pltpu.VMEM((2, HERE, n1, HD), BF16),
            pltpu.VMEM((N_Z, 2, GROUP * n0, HD), BF16),
            pltpu.VMEM((N_Z, 2, GROUP * n1, HD), BF16),
            pltpu.VMEM((ROWS, HD), BF16),
            pltpu.VMEM((32, PCAP), F32),
            pltpu.VMEM((N_Z, GROUP * n0), F32),
            pltpu.VMEM((N_Z, GROUP * n1), F32),
            pltpu.VMEM((ROWS, 1), F32),
            pltpu.VMEM((ROWS, 2 * HD), F32),
            pltpu.VMEM((GROUP, PCAP, HD), BF16),
            dma((3,)), dma, dma, dma((18,)), dma((18,)), dma((3,)), dma((3,)), dma((12,)), dma((12,)),
            dma((14,)), dma((14,)), dma((14,)), dma((14,)), dma((3,)), dma((3,)),
        ],
        compiler_params=pltpu.CompilerParams(
            vmem_limit_bytes=60 * 2**20, collective_id=0, has_side_effects=True
        ),
        name="patches",
    )(patch_bounds, byte_qkv.transpose(1, 0, 2), kv_weight)


def solution(mesh):
    return jax.shard_map(
        shards,
        mesh=mesh,
        in_specs=(P("ctx", None, "mp"), P(None, None, "mp"), P()),
        out_specs=P("ctx", "mp"),
        check_vma=False,
    )
```

```python
import math

import jax
import jax.numpy as jnp
from jax import lax
from jax.experimental import pallas as pl
from jax.experimental.pallas import tpu as pltpu
from jax.sharding import PartitionSpec as P

D = 4096
HEADS = 32
WIN = 16
HD = 128
BYTE_DEV = 512
EXT = BYTE_DEV + WIN
PCAP = 160
COLS = 512
HERE = 4
N_MP = 8
N_Z = 8
GROUP = 4
ROWS = GROUP * PCAP
SCALE = 1.0 / math.sqrt(HD)
SCALE2 = SCALE * math.log2(math.e)
EDGE = BYTE_DEV - 2 * WIN
MASKED = -1e30
F32 = jnp.float32
BF16 = jnp.bfloat16
CHUNKS = ((0, 64), (64, 96))
MESH = pl.DeviceIdType.MESH


def remote(src, dst, send, recv, where):
    return pltpu.make_async_remote_copy(
        src_ref=src, dst_ref=dst, send_sem=send, recv_sem=recv, device_id=where, device_id_type=MESH
    )


def kernel(
    bounds_hbm, bytes_hbm, weight_hbm, out_ref,
    bounds_ref, ext, tops, state, weight, plain, states, relay, acc, own0, own1, kv0, kv1,
    queries, live, bias0, bias1, top, mixed, outgoing,
    in_sem, halo_send, halo_recv, mp_send, mp_recv, q_send, q_recv, g_send, g_recv,
    up_send, up_recv, dn_send, dn_recv, o_send, o_recv,
):
    ctx = lax.axis_index("ctx")
    mp = lax.axis_index("mp")
    z = ctx // GROUP
    member = ctx % GROUP
    y = mp // 2
    xh = mp % 2
    owns, kvs, biases = (own0, own1), (kv0, kv1), (bias0, bias1)
    sent = []

    def at_mp(yy, xx):
        return lax.rem(yy + 4, 4) * 2 + xx

    def mate(k):
        return z * GROUP + lax.rem(member + k, GROUP)

    y_up, y_dn, x_other = at_mp(y + 1, xh), at_mp(y - 1, xh), at_mp(y, 1 - xh)
    far = at_mp(y + 2, xh)
    o_dn, o_up, o_far = at_mp(y - 1, 1 - xh), at_mp(y + 1, 1 - xh), at_mp(y + 2, 1 - xh)
    z_up = lax.rem(z + 1, N_Z) * GROUP + member
    z_dn = lax.rem(z + N_Z - 1, N_Z) * GROUP + member
    before_me = lax.rem(ctx + N_Z * GROUP - 1, N_Z * GROUP)
    after_me = lax.rem(ctx + 1, N_Z * GROUP)

    bounds_in = pltpu.make_async_copy(bounds_hbm, bounds_ref, in_sem.at[0])
    bytes_in = pltpu.make_async_copy(bytes_hbm, ext.at[:, pl.ds(0, BYTE_DEV)], in_sem.at[1])
    weight_in = pltpu.make_async_copy(weight_hbm, weight, in_sem.at[2])
    bounds_in.start()
    bytes_in.start()
    weight_in.start()

    barrier = pltpu.get_barrier_semaphore()
    partners = [{"ctx": before_me, "mp": mp}, {"ctx": after_me, "mp": mp},
                {"ctx": ctx, "mp": y_up}, {"ctx": ctx, "mp": y_dn}, {"ctx": mate(2), "mp": x_other},
                {"ctx": z_up, "mp": mp}, {"ctx": z_dn, "mp": mp}]
    partners += [{"ctx": mate(k), "mp": mp} for k in range(1, GROUP)]
    for partner in partners:
        pl.semaphore_signal(barrier, inc=1, device_id=partner, device_id_type=MESH)
    pl.semaphore_wait(barrier, len(partners))

    halo = remote(
        bytes_hbm.at[:, pl.ds(0, WIN)], ext.at[:, pl.ds(BYTE_DEV, WIN)], halo_send, halo_recv,
        {"ctx": before_me, "mp": mp},
    )
    halo.start()
    sent.append(halo)

    bounds_in.wait()
    row = bounds_ref[pl.ds(ctx, 1), :] - ctx * BYTE_DEV
    starts = row[:, :PCAP]
    ends = row[:, 1 : PCAP + 1]
    diag = lax.broadcasted_iota(jnp.int32, (PCAP, PCAP), 0) == lax.broadcasted_iota(
        jnp.int32, (PCAP, PCAP), 1
    )
    start_col = jnp.sum(jnp.where(diag, starts, 0), axis=1, keepdims=True)
    end_col = jnp.sum(jnp.where(diag, ends, 0), axis=1, keepdims=True)
    byte_col = lax.broadcasted_iota(jnp.int32, (EXT, PCAP), 0)
    inside_t = (byte_col >= starts) & (byte_col < ends)
    left = jnp.sum(jnp.where(inside_t, ends - byte_col, 0), axis=1, keepdims=True)

    def patch_tops(begin, end):
        room = left[begin:end]
        for h in range(HERE):
            cols = slice(h * HD, (h + 1) * HD)
            best = ext[0, begin:end, cols].astype(F32)
            for shift in (1, 2, 4, 8):
                later = pltpu.roll(best, end - begin - shift, 0)
                best = jnp.maximum(best, jnp.where(room > shift, later, -jnp.inf))
            tops[begin:end, cols] = best.astype(BF16)

    bytes_in.wait()
    patch_tops(0, BYTE_DEV)
    halo.wait_recv()
    patch_tops(EDGE, EXT)

    def cross(off, count):
        begin, end = start_col[off : off + count], end_col[off : off + count]
        byte_row = lax.broadcasted_iota(jnp.int32, (count, EXT), 1)
        inside = (byte_row >= begin) & (byte_row < end)
        first = ((byte_row == begin) & (end > begin)).astype(F32).astype(BF16)
        for h in range(HERE):
            cols = slice(h * HD, (h + 1) * HD)
            query = jnp.dot(first, tops[:, cols], preferred_element_type=F32).astype(BF16)
            scores = (
                lax.dot_general(
                    query, ext[1, :, cols], (((1,), (1,)), ((), ())), preferred_element_type=F32
                )
                * SCALE
            )
            scores = jnp.where(inside, scores, MASKED)
            scores = scores - jnp.max(scores, axis=1, keepdims=True)
            terms = jnp.where(inside, jnp.exp(scores), 0.0)
            total = jnp.sum(terms, axis=1, keepdims=True)
            weights = (terms / jnp.where(total > 0, total, 1.0)).astype(BF16)
            state[off : off + count, cols] = jnp.dot(
                weights, ext[2, :, cols], preferred_element_type=F32
            ).astype(BF16)

    def rows_of(c, part=None):
        off, count = CHUNKS[c]
        if part is None:
            return pl.ds(off, count)
        return pl.ds(off + part * (count // 2), count // 2)

    def hand(c, src, block, rows, slot, to):
        slot = 12 * c + slot
        return remote(src, states.at[block, rows], mp_send.at[slot], mp_recv.at[slot], {"ctx": ctx, "mp": to})

    def pass_on(c, block, part, slot, to, own=False):
        rows = rows_of(c, part)
        src = state.at[rows] if own else states.at[block, rows]
        copy = hand(c, src, block, rows, slot, to)
        copy.start()
        sent.append(copy)

    def arrived(c, block, part, slot):
        rows = rows_of(c, part)
        hand(c, states.at[block, rows], block, rows, slot, y_up).wait_recv()

    def x_hop(c, src, dst, slot, to):
        slot = 12 * c + slot
        return remote(src, dst, mp_send.at[slot], mp_recv.at[slot], {"ctx": mate(2), "mp": to})

    def hop(c, src, dst, slot, to):
        copy = x_hop(c, src, dst, slot, to)
        copy.start()
        sent.append(copy)

    def relay_on(c):
        for part, block, to in ((0, mp, x_other), (1, x_other, mp)):
            rows = rows_of(c, part)
            x_hop(c, relay.at[rows], relay.at[rows], 10 + part, to).wait_recv()
            hop(c, relay.at[rows], states.at[block, rows], 9 * part, to)

    def send_own(c):
        for part, to in ((0, mp), (1, x_other)):
            rows = rows_of(c, part)
            hop(c, state.at[rows], relay.at[rows], 10 + part, to)
        pass_on(c, mp, None, 1, y_up, True)
        pass_on(c, mp, None, 2, y_dn, True)

    def near(c):
        arrived(c, y_dn, None, 1)
        pass_on(c, y_dn, 0, 3, y_up)
        arrived(c, y_up, None, 2)
        pass_on(c, y_up, 1, 4, y_dn)

    def across(c):
        arrived(c, x_other, 0, 0)
        arrived(c, x_other, 1, 9)
        pass_on(c, x_other, None, 5, y_up)
        pass_on(c, x_other, None, 6, y_dn)

    def across_near(c):
        arrived(c, o_dn, None, 5)
        pass_on(c, o_dn, 0, 7, y_up)
        arrived(c, o_up, None, 6)
        pass_on(c, o_up, 1, 8, y_dn)

    def prepare(block):
        rows = pl.ds(pl.multiple_of(block * COLS, COLS), COLS)
        plain[block] = weight[rows].reshape(COLS, 2 * COLS)

    def project(c, block, first=False):
        rows = rows_of(c)
        part_rows = (state if first else states.at[block])[rows, :]
        part = jnp.dot(part_rows, plain[block], preferred_element_type=F32)
        if first:
            acc[rows, :] = part
        else:
            acc[rows, :] += part

    def exchange(c):
        off, count = CHUNKS[c]
        own, kv = owns[c], kvs[c]
        mine = pl.ds(pl.multiple_of(member * count, count), count)
        for part in range(2):
            for n in range(HERE):
                begin = part * COLS + n * HD
                own[part, n] = acc[off : off + count, begin : begin + HD].astype(BF16)
        copies = []
        for part in range(2):
            for k in range(1, GROUP):
                slot = 6 * c + part * 3 + k - 1
                copy = remote(
                    own.at[part, lax.rem(member + k, GROUP)], kv.at[z, part, mine],
                    g_send.at[slot], g_recv.at[slot], {"ctx": mate(k), "mp": mp},
                )
                copy.start()
                copies.append(copy)
                sent.append(copy)
            kv[z, part, mine, :] = own[part, member]
        return copies

    def piece(c, block, part, slot, up):
        block = lax.rem(block + N_Z, N_Z)
        slot = 7 * c + slot
        send, recv, to = (up_send, up_recv, z_up) if up else (dn_send, dn_recv, z_dn)
        ref = kvs[c].at[block, part]
        return remote(ref, ref, send.at[slot], recv.at[slot], {"ctx": to, "mp": mp})

    def ring_send(c, block, part, slot, up):
        copy = piece(c, block, part, slot, up)
        copy.start()
        sent.append(copy)

    def ring_start(c, copies):
        for part in range(2):
            for k in range(3):
                copies[part * 3 + k].wait_recv()
            ring_send(c, z, part, part, True)
            ring_send(c, z, part, part, False)

    def ring_hop(c, hop):
        for part in range(2):
            for up in (True, False):
                block = z - hop if up else z + hop
                if hop == 4 and part == (1 if up else 0):
                    continue
                slot = 2 * (hop - 1) + part if hop < 4 else 6
                piece(c, block, part, slot, up).wait_recv()
                if hop < 3:
                    ring_send(c, block, part, 2 * hop + part, up)
                elif hop == 3 and part == (0 if up else 1):
                    ring_send(c, block, part, 6, up)

    def attend(c, block, own, chunks=range(GROUP)):
        off, count = CHUNKS[c]
        keys_here = GROUP * count
        start = own and c == 0
        bias = biases[c][pl.ds(block, 1), :]
        keys = kvs[c][block, 0]
        values = jnp.concatenate([kvs[c][block, 1], jnp.ones((keys_here, HD), BF16)], axis=1)
        for i in chunks:
            rows = pl.ds(i * PCAP if isinstance(i, int) else pl.multiple_of(i * PCAP, PCAP), PCAP)
            scores = lax.dot_general(
                queries[rows, :], keys, (((1,), (1,)), ((), ())), preferred_element_type=F32
            ) + bias
            if own:
                at = lax.broadcasted_iota(jnp.int32, (1, keys_here), 1)
                slot = at + off
                for m in range(1, GROUP):
                    slot = slot + jnp.where(at >= m * count, PCAP - count, 0)
                query_at = lax.broadcasted_iota(jnp.int32, (PCAP, keys_here), 0) + i * PCAP
                scores = jnp.where(slot <= query_at, scores, MASKED)
            best = jnp.max(scores, axis=1, keepdims=True)
            if not start:
                before = top[rows, :]
                best = jnp.maximum(best, before)
                keep = jnp.exp2((before - best) * SCALE2)
            weights = jnp.exp2((scores - best) * SCALE2)
            part = jnp.dot(weights.astype(BF16), values, preferred_element_type=F32)
            if not start:
                part = mixed[rows, :] * keep + part
            mixed[rows, :] = part
            top[rows, :] = best

    def attend_hop(c, hop):
        def one(d, _):
            index = lax.rem(z + (2 * d - 1) * hop + N_Z, N_Z)

            @pl.when(index < z)
            def _():
                attend(c, index, False)

            return 0

        lax.fori_loop(0, 2 if hop < 4 else 1, one, 0)

    cross(*CHUNKS[0])
    send_own(0)
    cross(*CHUNKS[1])
    relay_on(0)
    send_own(1)
    weight_in.wait()
    near(0)
    prepare(mp)
    project(0, mp, True)
    prepare(y_dn)
    project(0, y_dn)
    across(0)
    relay_on(1)
    own_rows = pl.ds(pl.multiple_of(member * PCAP, PCAP), PCAP)
    q_copies = []
    for k in range(1, GROUP):
        head = lax.rem(member + k, GROUP)
        copy = remote(
            state.at[:, pl.ds(pl.multiple_of(head * HD, HD), HD)], queries.at[own_rows],
            q_send.at[k - 1], q_recv.at[k - 1], {"ctx": mate(k), "mp": mp},
        )
        copy.start()
        q_copies.append(copy)
        sent.append(copy)
    queries[own_rows, :] = state[:, pl.ds(pl.multiple_of(member * HD, HD), HD)]
    prepare(y_up)
    project(0, y_up)
    prepare(x_other)
    project(0, x_other)
    near(1)
    for block in (far, o_dn, o_up, o_far):
        prepare(block)
    arrived(0, far, 0, 3)
    arrived(0, far, 1, 4)
    project(0, far)
    across_near(0)
    across(1)
    project(0, o_dn)
    project(0, o_up)
    arrived(0, o_far, 0, 7)
    arrived(0, o_far, 1, 8)
    project(0, o_far)
    g0 = exchange(0)
    for n, block in enumerate((mp, y_dn, y_up, x_other)):
        project(1, block, n == 0)
    across_near(1)
    arrived(1, far, 0, 3)
    arrived(1, far, 1, 4)
    for block in (far, o_dn, o_up):
        project(1, block)
    ring_start(0, g0)

    bounds = bounds_ref[...]
    live[...] = jnp.where(bounds[:, 1 : PCAP + 1] > bounds[:, :PCAP], 0.0, MASKED)
    for c, (off, count) in enumerate(CHUNKS):
        for block in range(N_Z):
            biases[c][block : block + 1, :] = jnp.concatenate(
                [live[block * GROUP + i : block * GROUP + i + 1, off : off + count] for i in range(GROUP)],
                axis=1,
            )
    arrived(1, o_far, 0, 7)
    arrived(1, o_far, 1, 8)
    project(1, o_far)
    g1 = exchange(1)
    ring_hop(0, 1)
    for copy in q_copies:
        copy.wait_recv()
    attend(0, z, True)
    ring_start(1, g1)
    attend(1, z, True)
    attend_hop(0, 1)
    ring_hop(0, 2)
    attend_hop(0, 2)
    for c, number in ((1, 1), (0, 3), (1, 2), (0, 4), (1, 3)):
        ring_hop(c, number)
        attend_hop(c, number)
    ring_hop(1, 4)
    last = lax.rem(z + 4, N_Z)

    column = pl.ds(pl.multiple_of(member * HD, HD), HD)
    o_copies = []
    for k in (2, 1, 3, 0):
        index = lax.rem(member + k, GROUP)
        rows = pl.ds(pl.multiple_of(index * PCAP, PCAP), PCAP)

        @pl.when(last < z)
        def _():
            attend(1, last, False, (index,))

        dead = jnp.sum(jnp.where(diag, live[pl.ds(z * GROUP + index, 1), :], 0.0), axis=1, keepdims=True)
        value = jnp.where(dead < 0, 0.0, mixed[rows, :HD] / mixed[rows, HD:])
        outgoing[k] = (queries[rows, :].astype(F32) + value).astype(BF16)
        if k:
            copy = remote(
                outgoing.at[k], out_ref.at[:, column], o_send.at[k - 1], o_recv.at[k - 1],
                {"ctx": mate(k), "mp": mp},
            )
            copy.start()
            o_copies.append(copy)
            sent.append(copy)
    out_ref[:, column] = outgoing[0]
    for copy in o_copies:
        copy.wait_recv()
    for copy in sent:
        copy.wait_send()


def shards(byte_qkv, kv_weight, patch_bounds):
    anywhere = pl.BlockSpec(memory_space=pltpu.HBM)
    dma = pltpu.SemaphoreType.DMA
    (_, n0), (_, n1) = CHUNKS
    return pl.pallas_call(
        kernel,
        out_shape=pltpu.VMEM((PCAP, COLS), BF16),
        in_specs=[anywhere, anywhere, anywhere],
        out_specs=pl.BlockSpec(memory_space=pltpu.VMEM),
        scratch_shapes=[
            pltpu.VMEM((32, PCAP + 1), jnp.int32),
            pltpu.VMEM((3, EXT, COLS), BF16),
            pltpu.VMEM((EXT, COLS), BF16),
            pltpu.VMEM((PCAP, COLS), BF16),
            pltpu.VMEM((D, 2, COLS), BF16),
            pltpu.VMEM((N_MP, COLS, 2 * COLS), BF16),
            pltpu.VMEM((N_MP, PCAP, COLS), BF16),
            pltpu.VMEM((PCAP, COLS), BF16),
            pltpu.VMEM((PCAP, 2 * COLS), F32),
            pltpu.VMEM((2, HERE, n0, HD), BF16),
            pltpu.VMEM((2, HERE, n1, HD), BF16),
            pltpu.VMEM((N_Z, 2, GROUP * n0, HD), BF16),
            pltpu.VMEM((N_Z, 2, GROUP * n1, HD), BF16),
            pltpu.VMEM((ROWS, HD), BF16),
            pltpu.VMEM((32, PCAP), F32),
            pltpu.VMEM((N_Z, GROUP * n0), F32),
            pltpu.VMEM((N_Z, GROUP * n1), F32),
            pltpu.VMEM((ROWS, 1), F32),
            pltpu.VMEM((ROWS, 2 * HD), F32),
            pltpu.VMEM((GROUP, PCAP, HD), BF16),
            dma((3,)), dma, dma, dma((24,)), dma((24,)), dma((3,)), dma((3,)), dma((12,)), dma((12,)),
            dma((14,)), dma((14,)), dma((14,)), dma((14,)), dma((3,)), dma((3,)),
        ],
        compiler_params=pltpu.CompilerParams(
            vmem_limit_bytes=60 * 2**20, collective_id=0, has_side_effects=True
        ),
        name="patches",
    )(patch_bounds, byte_qkv.transpose(1, 0, 2), kv_weight)


def solution(mesh):
    return jax.shard_map(
        shards,
        mesh=mesh,
        in_specs=(P("ctx", None, "mp"), P(None, None, "mp"), P()),
        out_specs=P("ctx", "mp"),
        check_vma=False,
    )
```

```python
import math

import jax
import jax.numpy as jnp
from jax import lax
from jax.experimental import pallas as pl
from jax.experimental.pallas import tpu as pltpu
from jax.sharding import PartitionSpec as P

D = 4096
HEADS = 32
WIN = 16
HD = 128
BYTE_DEV = 512
EXT = BYTE_DEV + WIN
PCAP = 160
COLS = 512
HERE = 4
N_MP = 8
N_Z = 8
GROUP = 4
ROWS = GROUP * PCAP
SCALE = 1.0 / math.sqrt(HD)
SCALE2 = SCALE * math.log2(math.e)
EDGE = BYTE_DEV - 2 * WIN
MASKED = -1e30
F32 = jnp.float32
BF16 = jnp.bfloat16
CHUNKS = ((0, 64), (64, 96))
DIRECT = (0,)
MESH = pl.DeviceIdType.MESH


def remote(src, dst, send, recv, where):
    return pltpu.make_async_remote_copy(
        src_ref=src, dst_ref=dst, send_sem=send, recv_sem=recv, device_id=where, device_id_type=MESH
    )


def kernel(
    bounds_hbm, bytes_hbm, weight_hbm, out_ref,
    bounds_ref, ext, tops, state, weight, plain, states, relay, acc, own0, own1, kv0, kv1,
    queries, live, bias0, bias1, top, mixed, outgoing,
    in_sem, halo_send, halo_recv, mp_send, mp_recv, q_send, q_recv, g_send, g_recv,
    up_send, up_recv, dn_send, dn_recv, o_send, o_recv, d_send, d_recv,
):
    ctx = lax.axis_index("ctx")
    mp = lax.axis_index("mp")
    z = ctx // GROUP
    member = ctx % GROUP
    y = mp // 2
    xh = mp % 2
    owns, kvs, biases = (own0, own1), (kv0, kv1), (bias0, bias1)
    sent = []

    def at_mp(yy, xx):
        return lax.rem(yy + 4, 4) * 2 + xx

    def owner(plane, k):
        return lax.rem(plane + N_Z, N_Z) * GROUP + lax.rem(member + k, GROUP)

    def mate(k):
        return z * GROUP + lax.rem(member + k, GROUP)

    y_up, y_dn, x_other = at_mp(y + 1, xh), at_mp(y - 1, xh), at_mp(y, 1 - xh)
    far = at_mp(y + 2, xh)
    o_dn, o_up, o_far = at_mp(y - 1, 1 - xh), at_mp(y + 1, 1 - xh), at_mp(y + 2, 1 - xh)
    z_up = lax.rem(z + 1, N_Z) * GROUP + member
    z_dn = lax.rem(z + N_Z - 1, N_Z) * GROUP + member
    before_me = lax.rem(ctx + N_Z * GROUP - 1, N_Z * GROUP)
    after_me = lax.rem(ctx + 1, N_Z * GROUP)

    bounds_in = pltpu.make_async_copy(bounds_hbm, bounds_ref, in_sem.at[0])
    bytes_in = pltpu.make_async_copy(bytes_hbm, ext.at[:, pl.ds(0, BYTE_DEV)], in_sem.at[1])
    weight_in = pltpu.make_async_copy(weight_hbm, weight, in_sem.at[2])
    bounds_in.start()
    bytes_in.start()
    weight_in.start()

    barrier = pltpu.get_barrier_semaphore()
    partners = [{"ctx": before_me, "mp": mp}, {"ctx": after_me, "mp": mp},
                {"ctx": ctx, "mp": y_up}, {"ctx": ctx, "mp": y_dn}, {"ctx": mate(2), "mp": x_other},
                {"ctx": z_up, "mp": mp}, {"ctx": z_dn, "mp": mp}]
    partners += [{"ctx": mate(k), "mp": mp} for k in range(1, GROUP)]
    partners += [{"ctx": owner(plane, k), "mp": mp} for plane in (z + 1, z - 1) for k in range(1, GROUP)]
    for partner in partners:
        pl.semaphore_signal(barrier, inc=1, device_id=partner, device_id_type=MESH)
    pl.semaphore_wait(barrier, len(partners))

    halo = remote(
        bytes_hbm.at[:, pl.ds(0, WIN)], ext.at[:, pl.ds(BYTE_DEV, WIN)], halo_send, halo_recv,
        {"ctx": before_me, "mp": mp},
    )
    halo.start()
    sent.append(halo)

    bounds_in.wait()
    row = bounds_ref[pl.ds(ctx, 1), :] - ctx * BYTE_DEV
    starts = row[:, :PCAP]
    ends = row[:, 1 : PCAP + 1]
    diag = lax.broadcasted_iota(jnp.int32, (PCAP, PCAP), 0) == lax.broadcasted_iota(
        jnp.int32, (PCAP, PCAP), 1
    )
    start_col = jnp.sum(jnp.where(diag, starts, 0), axis=1, keepdims=True)
    end_col = jnp.sum(jnp.where(diag, ends, 0), axis=1, keepdims=True)
    byte_col = lax.broadcasted_iota(jnp.int32, (EXT, PCAP), 0)
    inside_t = (byte_col >= starts) & (byte_col < ends)
    left = jnp.sum(jnp.where(inside_t, ends - byte_col, 0), axis=1, keepdims=True)

    def patch_tops(begin, end):
        room = left[begin:end]
        for h in range(HERE):
            cols = slice(h * HD, (h + 1) * HD)
            best = ext[0, begin:end, cols].astype(F32)
            for shift in (1, 2, 4, 8):
                later = pltpu.roll(best, end - begin - shift, 0)
                best = jnp.maximum(best, jnp.where(room > shift, later, -jnp.inf))
            tops[begin:end, cols] = best.astype(BF16)

    bytes_in.wait()
    patch_tops(0, BYTE_DEV)
    halo.wait_recv()
    patch_tops(EDGE, EXT)

    def cross(off, count):
        begin, end = start_col[off : off + count], end_col[off : off + count]
        byte_row = lax.broadcasted_iota(jnp.int32, (count, EXT), 1)
        inside = (byte_row >= begin) & (byte_row < end)
        first = ((byte_row == begin) & (end > begin)).astype(F32).astype(BF16)
        for h in range(HERE):
            cols = slice(h * HD, (h + 1) * HD)
            query = jnp.dot(first, tops[:, cols], preferred_element_type=F32).astype(BF16)
            scores = (
                lax.dot_general(
                    query, ext[1, :, cols], (((1,), (1,)), ((), ())), preferred_element_type=F32
                )
                * SCALE
            )
            scores = jnp.where(inside, scores, MASKED)
            scores = scores - jnp.max(scores, axis=1, keepdims=True)
            terms = jnp.where(inside, jnp.exp(scores), 0.0)
            total = jnp.sum(terms, axis=1, keepdims=True)
            weights = (terms / jnp.where(total > 0, total, 1.0)).astype(BF16)
            state[off : off + count, cols] = jnp.dot(
                weights, ext[2, :, cols], preferred_element_type=F32
            ).astype(BF16)

    def rows_of(c, part=None):
        off, count = CHUNKS[c]
        if part is None:
            return pl.ds(off, count)
        return pl.ds(off + part * (count // 2), count // 2)

    def hand(c, src, block, rows, slot, to):
        slot = 12 * c + slot
        return remote(src, states.at[block, rows], mp_send.at[slot], mp_recv.at[slot], {"ctx": ctx, "mp": to})

    def pass_on(c, block, part, slot, to, own=False):
        rows = rows_of(c, part)
        src = state.at[rows] if own else states.at[block, rows]
        copy = hand(c, src, block, rows, slot, to)
        copy.start()
        sent.append(copy)

    def arrived(c, block, part, slot):
        rows = rows_of(c, part)
        hand(c, states.at[block, rows], block, rows, slot, y_up).wait_recv()

    def x_hop(c, src, dst, slot, to):
        slot = 12 * c + slot
        return remote(src, dst, mp_send.at[slot], mp_recv.at[slot], {"ctx": mate(2), "mp": to})

    def hop(c, src, dst, slot, to):
        copy = x_hop(c, src, dst, slot, to)
        copy.start()
        sent.append(copy)

    def relay_on(c):
        for part, block, to in ((0, mp, x_other), (1, x_other, mp)):
            rows = rows_of(c, part)
            x_hop(c, relay.at[rows], relay.at[rows], 10 + part, to).wait_recv()
            hop(c, relay.at[rows], states.at[block, rows], 9 * part, to)

    def send_own(c):
        for part, to in ((0, mp), (1, x_other)):
            rows = rows_of(c, part)
            hop(c, state.at[rows], relay.at[rows], 10 + part, to)
        pass_on(c, mp, None, 1, y_up, True)
        pass_on(c, mp, None, 2, y_dn, True)

    def near(c):
        arrived(c, y_dn, None, 1)
        pass_on(c, y_dn, 0, 3, y_up)
        arrived(c, y_up, None, 2)
        pass_on(c, y_up, 1, 4, y_dn)

    def across(c):
        arrived(c, x_other, 0, 0)
        arrived(c, x_other, 1, 9)
        pass_on(c, x_other, None, 5, y_up)
        pass_on(c, x_other, None, 6, y_dn)

    def across_near(c):
        arrived(c, o_dn, None, 5)
        pass_on(c, o_dn, 0, 7, y_up)
        arrived(c, o_up, None, 6)
        pass_on(c, o_up, 1, 8, y_dn)

    def prepare(block):
        rows = pl.ds(pl.multiple_of(block * COLS, COLS), COLS)
        plain[block] = weight[rows].reshape(COLS, 2 * COLS)

    def project(c, block, first=False):
        rows = rows_of(c)
        part_rows = (state if first else states.at[block])[rows, :]
        part = jnp.dot(part_rows, plain[block], preferred_element_type=F32)
        if first:
            acc[rows, :] = part
        else:
            acc[rows, :] += part

    def straight(c, block, part, k, way, src, rows):
        slot = 16 * c + 8 * way + 4 * part + k
        to = {"ctx": owner(z - 1 if way else z + 1, k), "mp": mp}
        return remote(src, kvs[c].at[block, part, rows], d_send.at[slot], d_recv.at[slot], to)

    def exchange(c):
        off, count = CHUNKS[c]
        own, kv = owns[c], kvs[c]
        mine = pl.ds(pl.multiple_of(member * count, count), count)
        for part in range(2):
            for n in range(HERE):
                begin = part * COLS + n * HD
                own[part, n] = acc[off : off + count, begin : begin + HD].astype(BF16)
        copies = []
        for part in range(2):
            if c in DIRECT:
                for k in (1, 2, 3, 0):
                    for way in range(2):
                        copy = straight(c, z, part, k, way, own.at[part, lax.rem(member + k, GROUP)], mine)
                        copy.start()
                        sent.append(copy)
            for k in range(1, GROUP):
                slot = 6 * c + part * 3 + k - 1
                copy = remote(
                    own.at[part, lax.rem(member + k, GROUP)], kv.at[z, part, mine],
                    g_send.at[slot], g_recv.at[slot], {"ctx": mate(k), "mp": mp},
                )
                copy.start()
                copies.append(copy)
                sent.append(copy)
            kv[z, part, mine, :] = own[part, member]
        return copies

    def piece(c, block, part, slot, up):
        block = lax.rem(block + N_Z, N_Z)
        slot = 7 * c + slot
        send, recv, to = (up_send, up_recv, z_up) if up else (dn_send, dn_recv, z_dn)
        ref = kvs[c].at[block, part]
        return remote(ref, ref, send.at[slot], recv.at[slot], {"ctx": to, "mp": mp})

    def ring_send(c, block, part, slot, up):
        copy = piece(c, block, part, slot, up)
        copy.start()
        sent.append(copy)

    def ring_start(c, copies):
        for part in range(2):
            for k in range(3):
                copies[part * 3 + k].wait_recv()
            if c not in DIRECT:
                ring_send(c, z, part, part, True)
                ring_send(c, z, part, part, False)

    def ring_hop(c, hop):
        for part in range(2):
            for up in (True, False):
                block = z - hop if up else z + hop
                if hop == 4 and part == (1 if up else 0):
                    continue
                slot = 2 * (hop - 1) + part if hop < 4 else 6
                if hop == 1 and c in DIRECT:
                    from_plane = lax.rem(block + N_Z, N_Z)
                    count = CHUNKS[c][1]
                    for k in range(GROUP):
                        first = lax.rem(member + GROUP - k, GROUP) * count
                        rows = pl.ds(pl.multiple_of(first, count), count)
                        ref = kvs[c].at[from_plane, part, rows]
                        straight(c, from_plane, part, k, 0 if up else 1, ref, rows).wait_recv()
                else:
                    piece(c, block, part, slot, up).wait_recv()
                if hop < 3:
                    ring_send(c, block, part, 2 * hop + part, up)
                elif hop == 3 and part == (0 if up else 1):
                    ring_send(c, block, part, 6, up)

    def attend(c, block, own, chunks=range(GROUP)):
        off, count = CHUNKS[c]
        keys_here = GROUP * count
        start = own and c == 0
        bias = biases[c][pl.ds(block, 1), :]
        keys = kvs[c][block, 0]
        values = jnp.concatenate([kvs[c][block, 1], jnp.ones((keys_here, HD), BF16)], axis=1)
        for i in chunks:
            rows = pl.ds(i * PCAP if isinstance(i, int) else pl.multiple_of(i * PCAP, PCAP), PCAP)
            scores = lax.dot_general(
                queries[rows, :], keys, (((1,), (1,)), ((), ())), preferred_element_type=F32
            ) + bias
            if own:
                at = lax.broadcasted_iota(jnp.int32, (1, keys_here), 1)
                slot = at + off
                for m in range(1, GROUP):
                    slot = slot + jnp.where(at >= m * count, PCAP - count, 0)
                query_at = lax.broadcasted_iota(jnp.int32, (PCAP, keys_here), 0) + i * PCAP
                scores = jnp.where(slot <= query_at, scores, MASKED)
            best = jnp.max(scores, axis=1, keepdims=True)
            if not start:
                before = top[rows, :]
                best = jnp.maximum(best, before)
                keep = jnp.exp2((before - best) * SCALE2)
            weights = jnp.exp2((scores - best) * SCALE2)
            part = jnp.dot(weights.astype(BF16), values, preferred_element_type=F32)
            if not start:
                part = mixed[rows, :] * keep + part
            mixed[rows, :] = part
            top[rows, :] = best

    def attend_hop(c, hop):
        def one(d, _):
            index = lax.rem(z + (2 * d - 1) * hop + N_Z, N_Z)

            @pl.when(index < z)
            def _():
                attend(c, index, False)

            return 0

        lax.fori_loop(0, 2 if hop < 4 else 1, one, 0)

    cross(*CHUNKS[0])
    send_own(0)
    cross(*CHUNKS[1])
    relay_on(0)
    send_own(1)
    weight_in.wait()
    near(0)
    prepare(mp)
    project(0, mp, True)
    prepare(y_dn)
    project(0, y_dn)
    across(0)
    relay_on(1)
    own_rows = pl.ds(pl.multiple_of(member * PCAP, PCAP), PCAP)
    q_copies = []
    for k in range(1, GROUP):
        head = lax.rem(member + k, GROUP)
        copy = remote(
            state.at[:, pl.ds(pl.multiple_of(head * HD, HD), HD)], queries.at[own_rows],
            q_send.at[k - 1], q_recv.at[k - 1], {"ctx": mate(k), "mp": mp},
        )
        copy.start()
        q_copies.append(copy)
        sent.append(copy)
    queries[own_rows, :] = state[:, pl.ds(pl.multiple_of(member * HD, HD), HD)]
    prepare(y_up)
    project(0, y_up)
    prepare(x_other)
    project(0, x_other)
    near(1)
    for block in (far, o_dn, o_up, o_far):
        prepare(block)

    bounds = bounds_ref[...]
    live[...] = jnp.where(bounds[:, 1 : PCAP + 1] > bounds[:, :PCAP], 0.0, MASKED)
    for c, (off, count) in enumerate(CHUNKS):
        for block in range(N_Z):
            biases[c][block : block + 1, :] = jnp.concatenate(
                [live[block * GROUP + i : block * GROUP + i + 1, off : off + count] for i in range(GROUP)],
                axis=1,
            )
    arrived(0, far, 0, 3)
    arrived(0, far, 1, 4)
    project(0, far)
    across_near(0)
    across(1)
    project(0, o_dn)
    project(0, o_up)
    arrived(0, o_far, 0, 7)
    arrived(0, o_far, 1, 8)
    project(0, o_far)
    g0 = exchange(0)
    for n, block in enumerate((mp, y_dn, y_up, x_other)):
        project(1, block, n == 0)
    arrived(1, far, 0, 3)
    arrived(1, far, 1, 4)
    project(1, far)
    if 0 not in DIRECT:
        ring_start(0, g0)
    across_near(1)
    project(1, o_dn)
    project(1, o_up)

    arrived(1, o_far, 0, 7)
    arrived(1, o_far, 1, 8)
    project(1, o_far)
    g1 = exchange(1)
    ring_hop(0, 1)
    for copy in q_copies:
        copy.wait_recv()
    if 0 in DIRECT:
        ring_start(0, g0)
    attend(0, z, True)
    ring_start(1, g1)
    attend(1, z, True)
    attend_hop(0, 1)
    ring_hop(0, 2)
    attend_hop(0, 2)
    for c, number in ((1, 1), (0, 3), (1, 2), (0, 4), (1, 3)):
        ring_hop(c, number)
        attend_hop(c, number)
    ring_hop(1, 4)
    last = lax.rem(z + 4, N_Z)

    column = pl.ds(pl.multiple_of(member * HD, HD), HD)
    o_copies = []
    for k in (2, 1, 3, 0):
        index = lax.rem(member + k, GROUP)
        rows = pl.ds(pl.multiple_of(index * PCAP, PCAP), PCAP)

        @pl.when(last < z)
        def _():
            attend(1, last, False, (index,))

        dead = jnp.sum(jnp.where(diag, live[pl.ds(z * GROUP + index, 1), :], 0.0), axis=1, keepdims=True)
        value = jnp.where(dead < 0, 0.0, mixed[rows, :HD] / mixed[rows, HD:])
        outgoing[k] = (queries[rows, :].astype(F32) + value).astype(BF16)
        if k:
            copy = remote(
                outgoing.at[k], out_ref.at[:, column], o_send.at[k - 1], o_recv.at[k - 1],
                {"ctx": mate(k), "mp": mp},
            )
            copy.start()
            o_copies.append(copy)
            sent.append(copy)
    out_ref[:, column] = outgoing[0]
    for copy in o_copies:
        copy.wait_recv()
    for copy in sent:
        copy.wait_send()


def shards(byte_qkv, kv_weight, patch_bounds):
    anywhere = pl.BlockSpec(memory_space=pltpu.HBM)
    dma = pltpu.SemaphoreType.DMA
    (_, n0), (_, n1) = CHUNKS
    return pl.pallas_call(
        kernel,
        out_shape=pltpu.VMEM((PCAP, COLS), BF16),
        in_specs=[anywhere, anywhere, anywhere],
        out_specs=pl.BlockSpec(memory_space=pltpu.VMEM),
        scratch_shapes=[
            pltpu.VMEM((32, PCAP + 1), jnp.int32),
            pltpu.VMEM((3, EXT, COLS), BF16),
            pltpu.VMEM((EXT, COLS), BF16),
            pltpu.VMEM((PCAP, COLS), BF16),
            pltpu.VMEM((D, 2, COLS), BF16),
            pltpu.VMEM((N_MP, COLS, 2 * COLS), BF16),
            pltpu.VMEM((N_MP, PCAP, COLS), BF16),
            pltpu.VMEM((PCAP, COLS), BF16),
            pltpu.VMEM((PCAP, 2 * COLS), F32),
            pltpu.VMEM((2, HERE, n0, HD), BF16),
            pltpu.VMEM((2, HERE, n1, HD), BF16),
            pltpu.VMEM((N_Z, 2, GROUP * n0, HD), BF16),
            pltpu.VMEM((N_Z, 2, GROUP * n1, HD), BF16),
            pltpu.VMEM((ROWS, HD), BF16),
            pltpu.VMEM((32, PCAP), F32),
            pltpu.VMEM((N_Z, GROUP * n0), F32),
            pltpu.VMEM((N_Z, GROUP * n1), F32),
            pltpu.VMEM((ROWS, 1), F32),
            pltpu.VMEM((ROWS, 2 * HD), F32),
            pltpu.VMEM((GROUP, PCAP, HD), BF16),
            dma((3,)), dma, dma, dma((24,)), dma((24,)), dma((3,)), dma((3,)), dma((12,)), dma((12,)),
            dma((14,)), dma((14,)), dma((14,)), dma((14,)), dma((3,)), dma((3,)), dma((32,)), dma((32,)),
        ],
        compiler_params=pltpu.CompilerParams(
            vmem_limit_bytes=60 * 2**20, collective_id=0, has_side_effects=True
        ),
        name="patches",
    )(patch_bounds, byte_qkv.transpose(1, 0, 2), kv_weight)


def solution(mesh):
    return jax.shard_map(
        shards,
        mesh=mesh,
        in_specs=(P("ctx", None, "mp"), P(None, None, "mp"), P()),
        out_specs=P("ctx", "mp"),
        check_vma=False,
    )
```

```python
import math

import jax
import jax.numpy as jnp
from jax import lax
from jax.experimental import pallas as pl
from jax.experimental.pallas import tpu as pltpu
from jax.sharding import PartitionSpec as P

D = 4096
HEADS = 32
WIN = 16
HD = 128
BYTE_DEV = 512
EXT = BYTE_DEV + WIN
PCAP = 160
COLS = 512
HERE = 4
N_MP = 8
N_Z = 8
GROUP = 4
ROWS = GROUP * PCAP
SCALE = 1.0 / math.sqrt(HD)
SCALE2 = SCALE * math.log2(math.e)
EDGE = BYTE_DEV - 2 * WIN
MASKED = -1e30
F32 = jnp.float32
BF16 = jnp.bfloat16
CHUNKS = ((0, 96), (96, 64))
DIRECT = (0,)
MESH = pl.DeviceIdType.MESH


def remote(src, dst, send, recv, where):
    return pltpu.make_async_remote_copy(
        src_ref=src, dst_ref=dst, send_sem=send, recv_sem=recv, device_id=where, device_id_type=MESH
    )


def kernel(
    bounds_hbm, bytes_hbm, weight_hbm, out_ref,
    bounds_ref, ext, tops, state, weight, plain, states, relay, acc, own0, own1, kv0, kv1,
    queries, live, bias0, bias1, top, mixed, outgoing,
    in_sem, halo_send, halo_recv, mp_send, mp_recv, q_send, q_recv, g_send, g_recv,
    up_send, up_recv, dn_send, dn_recv, o_send, o_recv, d_send, d_recv,
):
    ctx = lax.axis_index("ctx")
    mp = lax.axis_index("mp")
    z = ctx // GROUP
    member = ctx % GROUP
    y = mp // 2
    xh = mp % 2
    owns, kvs, biases = (own0, own1), (kv0, kv1), (bias0, bias1)
    sent = []

    def at_mp(yy, xx):
        return lax.rem(yy + 4, 4) * 2 + xx

    def owner(plane, k):
        return lax.rem(plane + N_Z, N_Z) * GROUP + lax.rem(member + k, GROUP)

    def mate(k):
        return z * GROUP + lax.rem(member + k, GROUP)

    y_up, y_dn, x_other = at_mp(y + 1, xh), at_mp(y - 1, xh), at_mp(y, 1 - xh)
    far = at_mp(y + 2, xh)
    o_dn, o_up, o_far = at_mp(y - 1, 1 - xh), at_mp(y + 1, 1 - xh), at_mp(y + 2, 1 - xh)
    z_up = lax.rem(z + 1, N_Z) * GROUP + member
    z_dn = lax.rem(z + N_Z - 1, N_Z) * GROUP + member
    before_me = lax.rem(ctx + N_Z * GROUP - 1, N_Z * GROUP)
    after_me = lax.rem(ctx + 1, N_Z * GROUP)

    bounds_in = pltpu.make_async_copy(bounds_hbm, bounds_ref, in_sem.at[0])
    bytes_in = pltpu.make_async_copy(bytes_hbm, ext.at[:, pl.ds(0, BYTE_DEV)], in_sem.at[1])
    weight_in = pltpu.make_async_copy(weight_hbm, weight, in_sem.at[2])
    bounds_in.start()
    bytes_in.start()
    weight_in.start()

    barrier = pltpu.get_barrier_semaphore()
    partners = [{"ctx": before_me, "mp": mp}, {"ctx": after_me, "mp": mp},
                {"ctx": ctx, "mp": y_up}, {"ctx": ctx, "mp": y_dn}, {"ctx": mate(2), "mp": x_other},
                {"ctx": z_up, "mp": mp}, {"ctx": z_dn, "mp": mp}]
    partners += [{"ctx": mate(k), "mp": mp} for k in range(1, GROUP)]
    partners += [{"ctx": owner(plane, k), "mp": mp} for plane in (z + 1, z - 1) for k in range(1, GROUP)]
    for partner in partners:
        pl.semaphore_signal(barrier, inc=1, device_id=partner, device_id_type=MESH)
    pl.semaphore_wait(barrier, len(partners))

    halo = remote(
        bytes_hbm.at[:, pl.ds(0, WIN)], ext.at[:, pl.ds(BYTE_DEV, WIN)], halo_send, halo_recv,
        {"ctx": before_me, "mp": mp},
    )
    halo.start()
    sent.append(halo)

    bounds_in.wait()
    row = bounds_ref[pl.ds(ctx, 1), :] - ctx * BYTE_DEV
    starts = row[:, :PCAP]
    ends = row[:, 1 : PCAP + 1]
    diag = lax.broadcasted_iota(jnp.int32, (PCAP, PCAP), 0) == lax.broadcasted_iota(
        jnp.int32, (PCAP, PCAP), 1
    )
    start_col = jnp.sum(jnp.where(diag, starts, 0), axis=1, keepdims=True)
    end_col = jnp.sum(jnp.where(diag, ends, 0), axis=1, keepdims=True)
    byte_col = lax.broadcasted_iota(jnp.int32, (EXT, PCAP), 0)
    inside_t = (byte_col >= starts) & (byte_col < ends)
    left = jnp.sum(jnp.where(inside_t, ends - byte_col, 0), axis=1, keepdims=True)

    def patch_tops(begin, end):
        room = left[begin:end]
        for h in range(HERE):
            cols = slice(h * HD, (h + 1) * HD)
            best = ext[0, begin:end, cols].astype(F32)
            for shift in (1, 2, 4, 8):
                later = pltpu.roll(best, end - begin - shift, 0)
                best = jnp.maximum(best, jnp.where(room > shift, later, -jnp.inf))
            tops[begin:end, cols] = best.astype(BF16)

    bytes_in.wait()
    patch_tops(0, BYTE_DEV)
    halo.wait_recv()
    patch_tops(EDGE, EXT)

    def cross(off, count):
        begin, end = start_col[off : off + count], end_col[off : off + count]
        byte_row = lax.broadcasted_iota(jnp.int32, (count, EXT), 1)
        inside = (byte_row >= begin) & (byte_row < end)
        first = ((byte_row == begin) & (end > begin)).astype(F32).astype(BF16)
        for h in range(HERE):
            cols = slice(h * HD, (h + 1) * HD)
            query = jnp.dot(first, tops[:, cols], preferred_element_type=F32).astype(BF16)
            scores = lax.dot_general(
                query, ext[1, :, cols], (((1,), (1,)), ((), ())), preferred_element_type=F32
            )
            scores = jnp.where(inside, scores, MASKED)
            terms = jnp.exp2((scores - jnp.max(scores, axis=1, keepdims=True)) * SCALE2)
            factor = jnp.where(end > begin, 1.0 / jnp.sum(terms, axis=1, keepdims=True), 0.0)
            weights = (terms * factor).astype(BF16)
            state[off : off + count, cols] = jnp.dot(
                weights, ext[2, :, cols], preferred_element_type=F32
            ).astype(BF16)

    def rows_of(c, part=None):
        off, count = CHUNKS[c]
        if part is None:
            return pl.ds(off, count)
        return pl.ds(off + part * (count // 2), count // 2)

    def hand(c, src, block, rows, slot, to):
        slot = 12 * c + slot
        return remote(src, states.at[block, rows], mp_send.at[slot], mp_recv.at[slot], {"ctx": ctx, "mp": to})

    def pass_on(c, block, part, slot, to, own=False):
        rows = rows_of(c, part)
        src = state.at[rows] if own else states.at[block, rows]
        copy = hand(c, src, block, rows, slot, to)
        copy.start()
        sent.append(copy)

    def arrived(c, block, part, slot):
        rows = rows_of(c, part)
        hand(c, states.at[block, rows], block, rows, slot, y_up).wait_recv()

    def x_hop(c, src, dst, slot, to):
        slot = 12 * c + slot
        return remote(src, dst, mp_send.at[slot], mp_recv.at[slot], {"ctx": mate(2), "mp": to})

    def hop(c, src, dst, slot, to):
        copy = x_hop(c, src, dst, slot, to)
        copy.start()
        sent.append(copy)

    def relay_on(c):
        for part, block, to in ((0, mp, x_other), (1, x_other, mp)):
            rows = rows_of(c, part)
            x_hop(c, relay.at[rows], relay.at[rows], 10 + part, to).wait_recv()
            hop(c, relay.at[rows], states.at[block, rows], 9 * part, to)

    def send_own(c):
        for part, to in ((0, mp), (1, x_other)):
            rows = rows_of(c, part)
            hop(c, state.at[rows], relay.at[rows], 10 + part, to)
        pass_on(c, mp, None, 1, y_up, True)
        pass_on(c, mp, None, 2, y_dn, True)

    def near(c):
        arrived(c, y_dn, None, 1)
        pass_on(c, y_dn, 0, 3, y_up)
        arrived(c, y_up, None, 2)
        pass_on(c, y_up, 1, 4, y_dn)

    def across(c):
        arrived(c, x_other, 0, 0)
        arrived(c, x_other, 1, 9)
        pass_on(c, x_other, None, 5, y_up)
        pass_on(c, x_other, None, 6, y_dn)

    def across_near(c):
        arrived(c, o_dn, None, 5)
        pass_on(c, o_dn, 0, 7, y_up)
        arrived(c, o_up, None, 6)
        pass_on(c, o_up, 1, 8, y_dn)

    def prepare(block):
        rows = pl.ds(pl.multiple_of(block * COLS, COLS), COLS)
        plain[block] = weight[rows].reshape(COLS, 2 * COLS)

    def project(c, block, first=False):
        rows = rows_of(c)
        part_rows = (state if first else states.at[block])[rows, :]
        part = jnp.dot(part_rows, plain[block], preferred_element_type=F32)
        if first:
            acc[rows, :] = part
        else:
            acc[rows, :] += part

    def straight(c, block, part, k, way, src, rows):
        slot = 16 * c + 8 * way + 4 * part + k
        to = {"ctx": owner(z - 1 if way else z + 1, k), "mp": mp}
        return remote(src, kvs[c].at[block, part, rows], d_send.at[slot], d_recv.at[slot], to)

    def exchange(c):
        off, count = CHUNKS[c]
        own, kv = owns[c], kvs[c]
        mine = pl.ds(pl.multiple_of(member * count, count), count)
        for part in range(2):
            for n in range(HERE):
                begin = part * COLS + n * HD
                own[part, n] = acc[off : off + count, begin : begin + HD].astype(BF16)
        copies = []
        for part in range(2):
            if c in DIRECT:
                for k in (1, 2, 3, 0):
                    for way in range(2):
                        copy = straight(c, z, part, k, way, own.at[part, lax.rem(member + k, GROUP)], mine)
                        copy.start()
                        sent.append(copy)
            for k in range(1, GROUP):
                slot = 6 * c + part * 3 + k - 1
                copy = remote(
                    own.at[part, lax.rem(member + k, GROUP)], kv.at[z, part, mine],
                    g_send.at[slot], g_recv.at[slot], {"ctx": mate(k), "mp": mp},
                )
                copy.start()
                copies.append(copy)
                sent.append(copy)
            kv[z, part, mine, :] = own[part, member]
        return copies

    def piece(c, block, part, slot, up):
        block = lax.rem(block + N_Z, N_Z)
        slot = 7 * c + slot
        send, recv, to = (up_send, up_recv, z_up) if up else (dn_send, dn_recv, z_dn)
        ref = kvs[c].at[block, part]
        return remote(ref, ref, send.at[slot], recv.at[slot], {"ctx": to, "mp": mp})

    def ring_send(c, block, part, slot, up):
        copy = piece(c, block, part, slot, up)
        copy.start()
        sent.append(copy)

    def ring_start(c, copies):
        for part in range(2):
            for k in range(3):
                copies[part * 3 + k].wait_recv()
            if c not in DIRECT:
                ring_send(c, z, part, part, True)
                ring_send(c, z, part, part, False)

    def ring_hop(c, hop):
        for part in range(2):
            for up in (True, False):
                block = z - hop if up else z + hop
                if hop == 4 and part == (1 if up else 0):
                    continue
                slot = 2 * (hop - 1) + part if hop < 4 else 6
                if hop == 1 and c in DIRECT:
                    from_plane = lax.rem(block + N_Z, N_Z)
                    count = CHUNKS[c][1]
                    for k in range(GROUP):
                        first = lax.rem(member + GROUP - k, GROUP) * count
                        rows = pl.ds(pl.multiple_of(first, count), count)
                        ref = kvs[c].at[from_plane, part, rows]
                        straight(c, from_plane, part, k, 0 if up else 1, ref, rows).wait_recv()
                else:
                    piece(c, block, part, slot, up).wait_recv()
                if hop < 3:
                    ring_send(c, block, part, 2 * hop + part, up)
                elif hop == 3 and part == (0 if up else 1):
                    ring_send(c, block, part, 6, up)

    def attend(c, block, own, chunks=range(GROUP)):
        off, count = CHUNKS[c]
        keys_here = GROUP * count
        start = own and c == 0
        bias = biases[c][pl.ds(block, 1), :]
        keys = kvs[c][block, 0]
        values = jnp.concatenate([kvs[c][block, 1], jnp.ones((keys_here, HD), BF16)], axis=1)
        for i in chunks:
            rows = pl.ds(i * PCAP if isinstance(i, int) else pl.multiple_of(i * PCAP, PCAP), PCAP)
            scores = lax.dot_general(
                queries[rows, :], keys, (((1,), (1,)), ((), ())), preferred_element_type=F32
            ) + bias
            if own:
                at = lax.broadcasted_iota(jnp.int32, (1, keys_here), 1)
                slot = at + off
                for m in range(1, GROUP):
                    slot = slot + jnp.where(at >= m * count, PCAP - count, 0)
                query_at = lax.broadcasted_iota(jnp.int32, (PCAP, keys_here), 0) + i * PCAP
                scores = jnp.where(slot <= query_at, scores, MASKED)
            best = jnp.max(scores, axis=1, keepdims=True)
            if not start:
                before = top[rows, :]
                best = jnp.maximum(best, before)
                keep = jnp.exp2((before - best) * SCALE2)
            weights = jnp.exp2((scores - best) * SCALE2)
            part = jnp.dot(weights.astype(BF16), values, preferred_element_type=F32)
            if not start:
                part = mixed[rows, :] * keep + part
            mixed[rows, :] = part
            top[rows, :] = best

    def attend_hop(c, hop):
        def one(d, _):
            index = lax.rem(z + (2 * d - 1) * hop + N_Z, N_Z)

            @pl.when(index < z)
            def _():
                attend(c, index, False)

            return 0

        lax.fori_loop(0, 2 if hop < 4 else 1, one, 0)

    cross(*CHUNKS[0])
    send_own(0)
    cross(*CHUNKS[1])
    relay_on(0)
    send_own(1)
    weight_in.wait()
    near(0)
    prepare(mp)
    project(0, mp, True)
    prepare(y_dn)
    project(0, y_dn)
    across(0)
    relay_on(1)
    own_rows = pl.ds(pl.multiple_of(member * PCAP, PCAP), PCAP)
    q_copies = []
    for k in range(1, GROUP):
        head = lax.rem(member + k, GROUP)
        copy = remote(
            state.at[:, pl.ds(pl.multiple_of(head * HD, HD), HD)], queries.at[own_rows],
            q_send.at[k - 1], q_recv.at[k - 1], {"ctx": mate(k), "mp": mp},
        )
        copy.start()
        q_copies.append(copy)
        sent.append(copy)
    queries[own_rows, :] = state[:, pl.ds(pl.multiple_of(member * HD, HD), HD)]
    prepare(y_up)
    project(0, y_up)
    prepare(x_other)
    project(0, x_other)
    near(1)
    for block in (far, o_dn, o_up, o_far):
        prepare(block)

    bounds = bounds_ref[...]
    live[...] = jnp.where(bounds[:, 1 : PCAP + 1] > bounds[:, :PCAP], 0.0, MASKED)
    for c, (off, count) in enumerate(CHUNKS):
        for block in range(N_Z):
            biases[c][block : block + 1, :] = jnp.concatenate(
                [live[block * GROUP + i : block * GROUP + i + 1, off : off + count] for i in range(GROUP)],
                axis=1,
            )
    arrived(0, far, 0, 3)
    arrived(0, far, 1, 4)
    project(0, far)
    across_near(0)
    across(1)
    project(0, o_dn)
    project(0, o_up)
    arrived(0, o_far, 0, 7)
    arrived(0, o_far, 1, 8)
    project(0, o_far)
    g0 = exchange(0)
    for n, block in enumerate((mp, y_dn, y_up, x_other)):
        project(1, block, n == 0)
    arrived(1, far, 0, 3)
    arrived(1, far, 1, 4)
    project(1, far)
    if 0 not in DIRECT:
        ring_start(0, g0)
    across_near(1)
    project(1, o_dn)
    project(1, o_up)

    arrived(1, o_far, 0, 7)
    arrived(1, o_far, 1, 8)
    project(1, o_far)
    g1 = exchange(1)
    ring_hop(0, 1)
    for copy in q_copies:
        copy.wait_recv()
    if 0 in DIRECT:
        ring_start(0, g0)
    attend(0, z, True)
    ring_start(1, g1)
    attend(1, z, True)
    attend_hop(0, 1)
    ring_hop(0, 2)
    attend_hop(0, 2)
    for c, number in ((1, 1), (0, 3), (1, 2), (0, 4), (1, 3)):
        ring_hop(c, number)
        attend_hop(c, number)
    ring_hop(1, 4)
    last = lax.rem(z + 4, N_Z)

    column = pl.ds(pl.multiple_of(member * HD, HD), HD)
    o_copies = []
    for k in (2, 1, 3, 0):
        index = lax.rem(member + k, GROUP)
        rows = pl.ds(pl.multiple_of(index * PCAP, PCAP), PCAP)

        @pl.when(last < z)
        def _():
            attend(1, last, False, (index,))

        dead = jnp.sum(jnp.where(diag, live[pl.ds(z * GROUP + index, 1), :], 0.0), axis=1, keepdims=True)
        value = jnp.where(dead < 0, 0.0, mixed[rows, :HD] / mixed[rows, HD:])
        outgoing[k] = (queries[rows, :].astype(F32) + value).astype(BF16)
        if k:
            copy = remote(
                outgoing.at[k], out_ref.at[:, column], o_send.at[k - 1], o_recv.at[k - 1],
                {"ctx": mate(k), "mp": mp},
            )
            copy.start()
            o_copies.append(copy)
            sent.append(copy)
    out_ref[:, column] = outgoing[0]
    for copy in o_copies:
        copy.wait_recv()
    for copy in sent:
        copy.wait_send()


def shards(byte_qkv, kv_weight, patch_bounds):
    anywhere = pl.BlockSpec(memory_space=pltpu.HBM)
    dma = pltpu.SemaphoreType.DMA
    (_, n0), (_, n1) = CHUNKS
    return pl.pallas_call(
        kernel,
        out_shape=pltpu.VMEM((PCAP, COLS), BF16),
        in_specs=[anywhere, anywhere, anywhere],
        out_specs=pl.BlockSpec(memory_space=pltpu.VMEM),
        scratch_shapes=[
            pltpu.VMEM((32, PCAP + 1), jnp.int32),
            pltpu.VMEM((3, EXT, COLS), BF16),
            pltpu.VMEM((EXT, COLS), BF16),
            pltpu.VMEM((PCAP, COLS), BF16),
            pltpu.VMEM((D, 2, COLS), BF16),
            pltpu.VMEM((N_MP, COLS, 2 * COLS), BF16),
            pltpu.VMEM((N_MP, PCAP, COLS), BF16),
            pltpu.VMEM((PCAP, COLS), BF16),
            pltpu.VMEM((PCAP, 2 * COLS), F32),
            pltpu.VMEM((2, HERE, n0, HD), BF16),
            pltpu.VMEM((2, HERE, n1, HD), BF16),
            pltpu.VMEM((N_Z, 2, GROUP * n0, HD), BF16),
            pltpu.VMEM((N_Z, 2, GROUP * n1, HD), BF16),
            pltpu.VMEM((ROWS, HD), BF16),
            pltpu.VMEM((32, PCAP), F32),
            pltpu.VMEM((N_Z, GROUP * n0), F32),
            pltpu.VMEM((N_Z, GROUP * n1), F32),
            pltpu.VMEM((ROWS, 1), F32),
            pltpu.VMEM((ROWS, 2 * HD), F32),
            pltpu.VMEM((GROUP, PCAP, HD), BF16),
            dma((3,)), dma, dma, dma((24,)), dma((24,)), dma((3,)), dma((3,)), dma((12,)), dma((12,)),
            dma((14,)), dma((14,)), dma((14,)), dma((14,)), dma((3,)), dma((3,)), dma((32,)), dma((32,)),
        ],
        compiler_params=pltpu.CompilerParams(
            vmem_limit_bytes=60 * 2**20, collective_id=0, has_side_effects=True
        ),
        name="patches",
    )(patch_bounds, byte_qkv.transpose(1, 0, 2), kv_weight)


def solution(mesh):
    return jax.shard_map(
        shards,
        mesh=mesh,
        in_specs=(P("ctx", None, "mp"), P(None, None, "mp"), P()),
        out_specs=P("ctx", "mp"),
        check_vma=False,
    )
```

```python
import math

import jax
import jax.numpy as jnp
from jax import lax
from jax.experimental import pallas as pl
from jax.experimental.pallas import tpu as pltpu
from jax.sharding import PartitionSpec as P

D = 4096
HEADS = 32
WIN = 16
HD = 128
BYTE_DEV = 512
EXT = BYTE_DEV + WIN
PCAP = 160
COLS = 512
HERE = 4
N_MP = 8
N_Z = 8
GROUP = 4
ROWS = GROUP * PCAP
SCALE = 1.0 / math.sqrt(HD)
SCALE2 = SCALE * math.log2(math.e)
EDGE = BYTE_DEV - 2 * WIN
MASKED = -1e30
F32 = jnp.float32
BF16 = jnp.bfloat16
CHUNKS = ((0, 96), (96, 64))
DIRECT = (0,)
MESH = pl.DeviceIdType.MESH


def remote(src, dst, send, recv, where):
    return pltpu.make_async_remote_copy(
        src_ref=src, dst_ref=dst, send_sem=send, recv_sem=recv, device_id=where, device_id_type=MESH
    )


def kernel(
    bounds_hbm, bytes_hbm, weight_hbm, out_ref,
    bounds_ref, ext, tops, state, weight, plain, states, relay, acc, own0, own1, kv0, kv1,
    queries, live, bias0, bias1, top, mixed, outgoing,
    in_sem, halo_send, halo_recv, mp_send, mp_recv, q_send, q_recv, g_send, g_recv,
    up_send, up_recv, dn_send, dn_recv, o_send, o_recv, d_send, d_recv,
):
    ctx = lax.axis_index("ctx")
    mp = lax.axis_index("mp")
    z = ctx // GROUP
    member = ctx % GROUP
    y = mp // 2
    xh = mp % 2
    owns, kvs, biases = (own0, own1), (kv0, kv1), (bias0, bias1)
    sent = []

    def at_mp(yy, xx):
        return lax.rem(yy + 4, 4) * 2 + xx

    def owner(plane, k):
        return lax.rem(plane + N_Z, N_Z) * GROUP + lax.rem(member + k, GROUP)

    def mate(k):
        return z * GROUP + lax.rem(member + k, GROUP)

    y_up, y_dn, x_other = at_mp(y + 1, xh), at_mp(y - 1, xh), at_mp(y, 1 - xh)
    far = at_mp(y + 2, xh)
    o_dn, o_up, o_far = at_mp(y - 1, 1 - xh), at_mp(y + 1, 1 - xh), at_mp(y + 2, 1 - xh)
    z_up = lax.rem(z + 1, N_Z) * GROUP + member
    z_dn = lax.rem(z + N_Z - 1, N_Z) * GROUP + member
    before_me = lax.rem(ctx + N_Z * GROUP - 1, N_Z * GROUP)
    after_me = lax.rem(ctx + 1, N_Z * GROUP)

    bounds_in = pltpu.make_async_copy(bounds_hbm, bounds_ref, in_sem.at[0])
    bytes_in = pltpu.make_async_copy(bytes_hbm, ext.at[:, pl.ds(0, BYTE_DEV)], in_sem.at[1])
    weight_in = pltpu.make_async_copy(weight_hbm, weight, in_sem.at[2])
    bounds_in.start()
    bytes_in.start()
    weight_in.start()

    barrier = pltpu.get_barrier_semaphore()
    partners = [{"ctx": before_me, "mp": mp}, {"ctx": after_me, "mp": mp},
                {"ctx": ctx, "mp": y_up}, {"ctx": ctx, "mp": y_dn}, {"ctx": mate(2), "mp": x_other},
                {"ctx": z_up, "mp": mp}, {"ctx": z_dn, "mp": mp}]
    partners += [{"ctx": mate(k), "mp": mp} for k in range(1, GROUP)]
    partners += [{"ctx": owner(plane, k), "mp": mp} for plane in (z + 1, z - 1) for k in range(1, GROUP)]
    for partner in partners:
        pl.semaphore_signal(barrier, inc=1, device_id=partner, device_id_type=MESH)
    pl.semaphore_wait(barrier, len(partners))

    halo = remote(
        bytes_hbm.at[:, pl.ds(0, WIN)], ext.at[:, pl.ds(BYTE_DEV, WIN)], halo_send, halo_recv,
        {"ctx": before_me, "mp": mp},
    )
    halo.start()
    sent.append(halo)

    bounds_in.wait()
    row = bounds_ref[pl.ds(ctx, 1), :] - ctx * BYTE_DEV
    starts = row[:, :PCAP]
    ends = row[:, 1 : PCAP + 1]
    diag = lax.broadcasted_iota(jnp.int32, (PCAP, PCAP), 0) == lax.broadcasted_iota(
        jnp.int32, (PCAP, PCAP), 1
    )
    start_col = jnp.sum(jnp.where(diag, starts, 0), axis=1, keepdims=True)
    end_col = jnp.sum(jnp.where(diag, ends, 0), axis=1, keepdims=True)
    byte_col = lax.broadcasted_iota(jnp.int32, (EXT, PCAP), 0)
    inside_t = (byte_col >= starts) & (byte_col < ends)
    left = jnp.sum(jnp.where(inside_t, ends - byte_col, 0), axis=1, keepdims=True)

    def patch_tops(begin, end):
        room = left[begin:end]
        for h in range(HERE):
            cols = slice(h * HD, (h + 1) * HD)
            best = ext[0, begin:end, cols].astype(F32)
            for shift in (1, 2, 4, 8):
                later = pltpu.roll(best, end - begin - shift, 0)
                best = jnp.maximum(best, jnp.where(room > shift, later, -jnp.inf))
            tops[begin:end, cols] = best.astype(BF16)

    bytes_in.wait()
    patch_tops(0, BYTE_DEV)
    halo.wait_recv()
    patch_tops(EDGE, EXT)

    def cross(off, count):
        begin, end = start_col[off : off + count], end_col[off : off + count]
        byte_row = lax.broadcasted_iota(jnp.int32, (count, EXT), 1)
        inside = (byte_row >= begin) & (byte_row < end)
        first = ((byte_row == begin) & (end > begin)).astype(F32).astype(BF16)
        for h in range(HERE):
            cols = slice(h * HD, (h + 1) * HD)
            query = jnp.dot(first, tops[:, cols], preferred_element_type=F32).astype(BF16)
            scores = lax.dot_general(
                query, ext[1, :, cols], (((1,), (1,)), ((), ())), preferred_element_type=F32
            )
            scores = jnp.where(inside, scores, MASKED)
            terms = jnp.exp2((scores - jnp.max(scores, axis=1, keepdims=True)) * SCALE2)
            factor = jnp.where(end > begin, 1.0 / jnp.sum(terms, axis=1, keepdims=True), 0.0)
            weights = (terms * factor).astype(BF16)
            state[off : off + count, cols] = jnp.dot(
                weights, ext[2, :, cols], preferred_element_type=F32
            ).astype(BF16)

    def rows_of(c, part=None):
        off, count = CHUNKS[c]
        if part is None:
            return pl.ds(off, count)
        return pl.ds(off + part * (count // 2), count // 2)

    def hand(c, src, block, rows, slot, to):
        slot = 12 * c + slot
        return remote(src, states.at[block, rows], mp_send.at[slot], mp_recv.at[slot], {"ctx": ctx, "mp": to})

    def pass_on(c, block, part, slot, to, own=False):
        rows = rows_of(c, part)
        src = state.at[rows] if own else states.at[block, rows]
        copy = hand(c, src, block, rows, slot, to)
        copy.start()
        sent.append(copy)

    def arrived(c, block, part, slot):
        rows = rows_of(c, part)
        hand(c, states.at[block, rows], block, rows, slot, y_up).wait_recv()

    def x_hop(c, src, dst, slot, to):
        slot = 12 * c + slot
        return remote(src, dst, mp_send.at[slot], mp_recv.at[slot], {"ctx": mate(2), "mp": to})

    def hop(c, src, dst, slot, to):
        copy = x_hop(c, src, dst, slot, to)
        copy.start()
        sent.append(copy)

    def relay_on(c):
        for part, block, to in ((0, mp, x_other), (1, x_other, mp)):
            rows = rows_of(c, part)
            x_hop(c, relay.at[rows], relay.at[rows], 10 + part, to).wait_recv()
            hop(c, relay.at[rows], states.at[block, rows], 9 * part, to)

    def send_own(c):
        for part, to in ((0, mp), (1, x_other)):
            rows = rows_of(c, part)
            hop(c, state.at[rows], relay.at[rows], 10 + part, to)
        pass_on(c, mp, None, 1, y_up, True)
        pass_on(c, mp, None, 2, y_dn, True)

    def near(c):
        arrived(c, y_dn, None, 1)
        pass_on(c, y_dn, 0, 3, y_up)
        arrived(c, y_up, None, 2)
        pass_on(c, y_up, 1, 4, y_dn)

    def across(c):
        arrived(c, x_other, 0, 0)
        arrived(c, x_other, 1, 9)
        pass_on(c, x_other, None, 5, y_up)
        pass_on(c, x_other, None, 6, y_dn)

    def across_near(c):
        arrived(c, o_dn, None, 5)
        pass_on(c, o_dn, 0, 7, y_up)
        arrived(c, o_up, None, 6)
        pass_on(c, o_up, 1, 8, y_dn)

    def prepare(block):
        rows = pl.ds(pl.multiple_of(block * COLS, COLS), COLS)
        plain[block] = weight[rows].reshape(COLS, 2 * COLS)

    def project(c, block, first=False):
        rows = rows_of(c)
        part_rows = (state if first else states.at[block])[rows, :]
        part = jnp.dot(part_rows, plain[block], preferred_element_type=F32)
        if first:
            acc[rows, :] = part
        else:
            acc[rows, :] += part

    def straight(c, block, part, k, way, src, rows):
        slot = 16 * c + 8 * way + 4 * part + k
        to = {"ctx": owner(z - 1 if way else z + 1, k), "mp": mp}
        return remote(src, kvs[c].at[block, part, rows], d_send.at[slot], d_recv.at[slot], to)

    def exchange(c):
        off, count = CHUNKS[c]
        own, kv = owns[c], kvs[c]
        mine = pl.ds(pl.multiple_of(member * count, count), count)
        for part in range(2):
            for n in range(HERE):
                begin = part * COLS + n * HD
                own[part, n] = acc[off : off + count, begin : begin + HD].astype(BF16)
        copies = []
        if c in DIRECT:
            for part in range(2):
                for k in (1, 2, 3, 0):
                    for way in range(2):
                        copy = straight(c, z, part, k, way, own.at[part, lax.rem(member + k, GROUP)], mine)
                        copy.start()
                        sent.append(copy)
        for part in range(2):
            for k in range(1, GROUP):
                slot = 6 * c + part * 3 + k - 1
                copy = remote(
                    own.at[part, lax.rem(member + k, GROUP)], kv.at[z, part, mine],
                    g_send.at[slot], g_recv.at[slot], {"ctx": mate(k), "mp": mp},
                )
                copy.start()
                copies.append(copy)
                sent.append(copy)
            kv[z, part, mine, :] = own[part, member]
        return copies

    def piece(c, block, part, slot, up):
        block = lax.rem(block + N_Z, N_Z)
        slot = 7 * c + slot
        send, recv, to = (up_send, up_recv, z_up) if up else (dn_send, dn_recv, z_dn)
        ref = kvs[c].at[block, part]
        return remote(ref, ref, send.at[slot], recv.at[slot], {"ctx": to, "mp": mp})

    def ring_send(c, block, part, slot, up):
        copy = piece(c, block, part, slot, up)
        copy.start()
        sent.append(copy)

    def ring_start(c, copies):
        for part in range(2):
            for k in range(3):
                copies[part * 3 + k].wait_recv()
            if c not in DIRECT:
                ring_send(c, z, part, part, True)
                ring_send(c, z, part, part, False)

    def ring_hop(c, hop):
        for part in range(2):
            for up in (True, False):
                block = z - hop if up else z + hop
                if hop == 4 and part == (1 if up else 0):
                    continue
                slot = 2 * (hop - 1) + part if hop < 4 else 6
                if hop == 1 and c in DIRECT:
                    from_plane = lax.rem(block + N_Z, N_Z)
                    count = CHUNKS[c][1]
                    for k in range(GROUP):
                        first = lax.rem(member + GROUP - k, GROUP) * count
                        rows = pl.ds(pl.multiple_of(first, count), count)
                        ref = kvs[c].at[from_plane, part, rows]
                        straight(c, from_plane, part, k, 0 if up else 1, ref, rows).wait_recv()
                else:
                    piece(c, block, part, slot, up).wait_recv()
                if hop < 3:
                    ring_send(c, block, part, 2 * hop + part, up)
                elif hop == 3 and part == (0 if up else 1):
                    ring_send(c, block, part, 6, up)

    def attend(c, block, own, chunks=range(GROUP)):
        off, count = CHUNKS[c]
        keys_here = GROUP * count
        start = own and c == 0
        bias = biases[c][pl.ds(block, 1), :]
        keys = kvs[c][block, 0]
        values = jnp.concatenate([kvs[c][block, 1], jnp.ones((keys_here, HD), BF16)], axis=1)
        for i in chunks:
            rows = pl.ds(i * PCAP if isinstance(i, int) else pl.multiple_of(i * PCAP, PCAP), PCAP)
            scores = lax.dot_general(
                queries[rows, :], keys, (((1,), (1,)), ((), ())), preferred_element_type=F32
            ) + bias
            if own:
                at = lax.broadcasted_iota(jnp.int32, (1, keys_here), 1)
                slot = at + off
                for m in range(1, GROUP):
                    slot = slot + jnp.where(at >= m * count, PCAP - count, 0)
                query_at = lax.broadcasted_iota(jnp.int32, (PCAP, keys_here), 0) + i * PCAP
                scores = jnp.where(slot <= query_at, scores, MASKED)
            best = jnp.max(scores, axis=1, keepdims=True)
            if not start:
                before = top[rows, :]
                best = jnp.maximum(best, before)
                keep = jnp.exp2((before - best) * SCALE2)
            weights = jnp.exp2((scores - best) * SCALE2)
            part = jnp.dot(weights.astype(BF16), values, preferred_element_type=F32)
            if not start:
                part = mixed[rows, :] * keep + part
            mixed[rows, :] = part
            top[rows, :] = best

    def attend_hop(c, hop):
        def one(d, _):
            index = lax.rem(z + (2 * d - 1) * hop + N_Z, N_Z)

            @pl.when(index < z)
            def _():
                attend(c, index, False)

            return 0

        lax.fori_loop(0, 2 if hop < 4 else 1, one, 0)

    cross(*CHUNKS[0])
    send_own(0)
    cross(*CHUNKS[1])
    relay_on(0)
    send_own(1)
    weight_in.wait()
    near(0)
    prepare(mp)
    project(0, mp, True)
    prepare(y_dn)
    project(0, y_dn)
    across(0)
    relay_on(1)
    own_rows = pl.ds(pl.multiple_of(member * PCAP, PCAP), PCAP)
    q_copies = []
    for k in range(1, GROUP):
        head = lax.rem(member + k, GROUP)
        copy = remote(
            state.at[:, pl.ds(pl.multiple_of(head * HD, HD), HD)], queries.at[own_rows],
            q_send.at[k - 1], q_recv.at[k - 1], {"ctx": mate(k), "mp": mp},
        )
        copy.start()
        q_copies.append(copy)
        sent.append(copy)
    queries[own_rows, :] = state[:, pl.ds(pl.multiple_of(member * HD, HD), HD)]
    prepare(y_up)
    project(0, y_up)
    prepare(x_other)
    project(0, x_other)
    near(1)
    for block in (far, o_dn, o_up, o_far):
        prepare(block)

    bounds = bounds_ref[...]
    live[...] = jnp.where(bounds[:, 1 : PCAP + 1] > bounds[:, :PCAP], 0.0, MASKED)
    for c, (off, count) in enumerate(CHUNKS):
        for block in range(N_Z):
            biases[c][block : block + 1, :] = jnp.concatenate(
                [live[block * GROUP + i : block * GROUP + i + 1, off : off + count] for i in range(GROUP)],
                axis=1,
            )
    arrived(0, far, 0, 3)
    arrived(0, far, 1, 4)
    project(0, far)
    across_near(0)
    across(1)
    project(0, o_dn)
    project(0, o_up)
    arrived(0, o_far, 0, 7)
    arrived(0, o_far, 1, 8)
    project(0, o_far)
    g0 = exchange(0)
    for n, block in enumerate((mp, y_dn, y_up, x_other)):
        project(1, block, n == 0)
    arrived(1, far, 0, 3)
    arrived(1, far, 1, 4)
    project(1, far)
    if 0 not in DIRECT:
        ring_start(0, g0)
    across_near(1)
    project(1, o_dn)
    project(1, o_up)

    arrived(1, o_far, 0, 7)
    arrived(1, o_far, 1, 8)
    project(1, o_far)
    g1 = exchange(1)
    ring_hop(0, 1)
    for copy in q_copies:
        copy.wait_recv()
    if 0 in DIRECT:
        ring_start(0, g0)
    attend(0, z, True)
    ring_start(1, g1)
    attend(1, z, True)
    attend_hop(0, 1)
    ring_hop(0, 2)
    attend_hop(0, 2)
    for c, number in ((1, 1), (0, 3), (1, 2), (0, 4), (1, 3)):
        ring_hop(c, number)
        attend_hop(c, number)
    ring_hop(1, 4)
    last = lax.rem(z + 4, N_Z)

    column = pl.ds(pl.multiple_of(member * HD, HD), HD)
    o_copies = []
    for k in (2, 1, 3, 0):
        index = lax.rem(member + k, GROUP)
        rows = pl.ds(pl.multiple_of(index * PCAP, PCAP), PCAP)

        @pl.when(last < z)
        def _():
            attend(1, last, False, (index,))

        dead = jnp.sum(jnp.where(diag, live[pl.ds(z * GROUP + index, 1), :], 0.0), axis=1, keepdims=True)
        value = jnp.where(dead < 0, 0.0, mixed[rows, :HD] / mixed[rows, HD:])
        outgoing[k] = (queries[rows, :].astype(F32) + value).astype(BF16)
        if k:
            copy = remote(
                outgoing.at[k], out_ref.at[:, column], o_send.at[k - 1], o_recv.at[k - 1],
                {"ctx": mate(k), "mp": mp},
            )
            copy.start()
            o_copies.append(copy)
            sent.append(copy)
    out_ref[:, column] = outgoing[0]
    for copy in o_copies:
        copy.wait_recv()
    for copy in sent:
        copy.wait_send()


def shards(byte_qkv, kv_weight, patch_bounds):
    anywhere = pl.BlockSpec(memory_space=pltpu.HBM)
    dma = pltpu.SemaphoreType.DMA
    (_, n0), (_, n1) = CHUNKS
    return pl.pallas_call(
        kernel,
        out_shape=pltpu.VMEM((PCAP, COLS), BF16),
        in_specs=[anywhere, anywhere, anywhere],
        out_specs=pl.BlockSpec(memory_space=pltpu.VMEM),
        scratch_shapes=[
            pltpu.VMEM((32, PCAP + 1), jnp.int32),
            pltpu.VMEM((3, EXT, COLS), BF16),
            pltpu.VMEM((EXT, COLS), BF16),
            pltpu.VMEM((PCAP, COLS), BF16),
            pltpu.VMEM((D, 2, COLS), BF16),
            pltpu.VMEM((N_MP, COLS, 2 * COLS), BF16),
            pltpu.VMEM((N_MP, PCAP, COLS), BF16),
            pltpu.VMEM((PCAP, COLS), BF16),
            pltpu.VMEM((PCAP, 2 * COLS), F32),
            pltpu.VMEM((2, HERE, n0, HD), BF16),
            pltpu.VMEM((2, HERE, n1, HD), BF16),
            pltpu.VMEM((N_Z, 2, GROUP * n0, HD), BF16),
            pltpu.VMEM((N_Z, 2, GROUP * n1, HD), BF16),
            pltpu.VMEM((ROWS, HD), BF16),
            pltpu.VMEM((32, PCAP), F32),
            pltpu.VMEM((N_Z, GROUP * n0), F32),
            pltpu.VMEM((N_Z, GROUP * n1), F32),
            pltpu.VMEM((ROWS, 1), F32),
            pltpu.VMEM((ROWS, 2 * HD), F32),
            pltpu.VMEM((GROUP, PCAP, HD), BF16),
            dma((3,)), dma, dma, dma((24,)), dma((24,)), dma((3,)), dma((3,)), dma((12,)), dma((12,)),
            dma((14,)), dma((14,)), dma((14,)), dma((14,)), dma((3,)), dma((3,)), dma((32,)), dma((32,)),
        ],
        compiler_params=pltpu.CompilerParams(
            vmem_limit_bytes=60 * 2**20, collective_id=0, has_side_effects=True
        ),
        name="patches",
    )(patch_bounds, byte_qkv.transpose(1, 0, 2), kv_weight)


def solution(mesh):
    return jax.shard_map(
        shards,
        mesh=mesh,
        in_specs=(P("ctx", None, "mp"), P(None, None, "mp"), P()),
        out_specs=P("ctx", "mp"),
        check_vma=False,
    )
```
